768 devices in a mesh: dom: 192 (over z, y, core), sub: 4 (over x).
Axes of the slice: x: 4, y: 8, z: 12, core: 2. Of those that a mesh axis runs over, the one named last changes fastest.
Arguments:
- rhs: float32 [2, 589824], P(None, ('dom', 'sub')), may hold values from -6 to 6
- start: float32 [2, 589824], P(None, ('dom', 'sub')), may hold values from -6 to 6
- stiffness: bfloat16 [589824, 768], P(('dom', 'sub')), may hold values from -0.109375 to 0.109375
- local_inverse: bfloat16 [589824, 768], P(('dom', 'sub')), may hold values from -0.109375 to 0.109375
- basis: bfloat16 [24, 589824], P(None, ('dom', 'sub')), may hold values from -0.21875 to 0.21875
- weights: float32 [589824], P(('dom', 'sub')), may hold values from 0.3 to 1
- coarse_inverse: float32 [18432, 18432], P(('dom', 'sub')), may hold values from -0.1875 to 0.1875
- orders: int32 [768], P(('dom', 'sub')), may hold values from 192 to 768, as said below
- out_rows: int32 [768, 6, 128], P(('dom', 'sub')), may hold values from 0 to 191
- out_counts: int32 [768, 6], P(('dom', 'sub')), may hold values from 0 to 128, as said below
- in_rows: int32 [768, 6, 128], P(('dom', 'sub')), may hold values from 0 to 191
Outputs:
- solution: float32 [2, 589824], P(None, ('dom', 'sub'))
- residual: float32 [2, 589824], P(None, ('dom', 'sub'))
The draws below stay inside these ranges and needn't reach their ends.
Inputs may be any that keep to these rules, and one draw needn't show every extreme that they name: `orders`: some subdomain has order exactly 768, another exactly 192. `out_rows`: every listed row lies below every subdomain's order. `in_rows`: every listed row lies below every subdomain's order. `out_counts`: some direction of some subdomain uses all 128 slots.
All inputs are finite; a program needn't handle non-finite values.
Results may differ from the reference program's by a relative error of at most 0.0019.
Values sent between devices are 32-bit elements; how exact they have to be, the bound alone decides.
No kernel may reach another device: no remote copies, remote signals or barrier semaphores. Data moves between devices by JAX's collectives and lax.ppermute only.
A program may use at most 32 MiB of HBM per device.

```python
import jax
import jax.numpy as jnp
from jax import lax

SUB_N = 768
NV = 24
H = 128
LOADS = 2
ITERS = 1
DOMAINS = 768
ROWS = 589824
NC = 18432
N_DOM = 192
N_SUB = 4


def draw_orders(key, part):
    orders_drawn = jax.random.randint(key, (DOMAINS,), SUB_N // 4, SUB_N + 1)
    chosen = jax.random.randint(jax.random.fold_in(key, 7), (), 0, DOMAINS)
    orders_drawn = orders_drawn.at[chosen].set(SUB_N)
    orders_drawn = orders_drawn.at[(chosen + 1) % DOMAINS].set(SUB_N // 4)
    return orders_drawn.astype(jnp.int32)


def draw_out_counts(key, part):
    counts_drawn = jax.random.randint(key, (DOMAINS, 6), 0, H + 1)
    chosen = jax.random.randint(jax.random.fold_in(key, 11), (), 0, DOMAINS)
    counts_drawn = counts_drawn.at[chosen, 0].set(H)
    return counts_drawn.astype(jnp.int32)


def touch_ends(result, own_key, least, top_value):
    longest = result.shape.index(max(result.shape))
    spots = []
    for shift in (0, 1):
        where = [jax.random.randint(jax.random.fold_in(own_key, axis), (), 0, length) for axis, length in enumerate(result.shape)]
        where[longest] = (where[longest] + shift) % result.shape[longest]
        spots.append(tuple(where))
    return result.at[spots[0]].set(least).at[spots[1]].set(top_value)


def raised(values, own_key, source, target, shards_of, factor):
    def block_of(dim):
        return (jnp.arange(values.shape[dim]) // (values.shape[dim] // shards_of)).reshape((-1,) + (1,) * (values.ndim - 1 - dim))

    near = jax.random.permutation(own_key, shards_of)[block_of(target)]
    other_side = (block_of(target) + shards_of // 2) % shards_of
    return jnp.where((block_of(source) == near) | (block_of(source) == other_side), factor * values, values)


def steps_of(stream_key, extent, shards, low, top_value):
    gain, own = 1.0, jax.random.fold_in(stream_key, 6)
    for dim, blocks in shards:
        heights = jnp.exp(jax.random.uniform(jax.random.fold_in(own, dim), (blocks,), jnp.float32, low / len(shards), top_value / len(shards)))
        gain = gain * jnp.repeat(heights, extent[dim] // blocks).reshape([-1 if axis == dim else 1 for axis in range(len(extent))])
    return gain


def centred(stream_key, shape, width, limit, split=(), dtype=jnp.bfloat16):
    drawn = jax.random.normal(stream_key, shape, jnp.float32) * width
    if len(split) > 0:
        drawn = steps_of(stream_key, shape, split, -0.22, 0.18) * drawn
    return jnp.clip(drawn, min=-limit, max=limit).astype(dtype)


def noise_with(rng, dims, deviation, bound, pieces, heavy, dtype=jnp.bfloat16):
    array = deviation * jax.random.normal(rng, dims, jnp.float32)
    if pieces:
        array = array * steps_of(rng, dims, pieces, -0.22, 0.18)
    return jnp.clip(raised(array, jax.random.fold_in(rng, 3), *heavy), -bound, bound).astype(dtype)


def setup_inputs(seed: int = 0) -> dict:
    key_of = jax.random.split(jax.random.key(seed), 12)
    return {
        "rhs": centred(key_of[0], (LOADS, ROWS), 1.0, 6.0, ((1, 768),), jnp.float32),
        "start": centred(key_of[1], (LOADS, ROWS), 1.0, 6.0, ((1, 768),), jnp.float32),
        "stiffness": centred(key_of[2], (ROWS, SUB_N), (4 * SUB_N) ** -0.5, 0.109375, ((0, 768),)),
        "local_inverse": centred(key_of[3], (ROWS, SUB_N), (4 * SUB_N) ** -0.5, 0.109375, ((0, 768),)),
        "basis": centred(key_of[4], (NV, ROWS), SUB_N ** -0.5, 0.21875, ((1, 768),)),
        "weights": jnp.clip(0.3 + 0.7 * jax.random.uniform(key_of[5], (ROWS,), jnp.float32) ** steps_of(key_of[5], (ROWS,), ((0, 768),), -0.2, 0.2), 0.3, 1.0),
        "coarse_inverse": noise_with(key_of[6], (NC, NC), NC ** -0.5, 0.1875, ((0, 768),), (1, 0, 768, 6.0), jnp.float32),
        "orders": draw_orders(jax.random.fold_in(key_of[11], 71), 0),
        "out_rows": touch_ends(jax.random.randint(key_of[8], (DOMAINS, 6, H), 0, SUB_N // 4), jax.random.fold_in(key_of[8], 1), 0, (SUB_N // 4) - 1).astype(jnp.int32),
        "out_counts": draw_out_counts(jax.random.fold_in(key_of[11], 71), 0),
        "in_rows": touch_ends(jax.random.randint(key_of[10], (DOMAINS, 6, H), 0, SUB_N // 4), jax.random.fold_in(key_of[10], 1), 0, (SUB_N // 4) - 1).astype(jnp.int32),
    }


DIRECTIONS = (("sub", 1), ("sub", -1), ("dom", 1), ("dom", -1), ("dom", 2), ("dom", -2))


def shifted(grid, axis_pos, offset):
    moved = jnp.roll(grid, offset, axis=axis_pos)
    length = grid.shape[axis_pos]
    where_from = jnp.arange(length) - offset
    valid = (where_from >= 0) & (where_from < length)
    if axis_pos == 0:
        valid = valid[:, None, None, None]
    else:
        valid = valid[None, :, None, None]
    return jnp.where(valid, moved, jnp.zeros_like(moved))


def add_rows(summed, rows_here, arrived):
    return summed.at[:, rows_here].add(arrived)


def assemble(terms, out_rows, out_counts, in_rows):
    slot_ids = jnp.arange(H)
    summed = terms
    for index_dir, (axis_name, offset) in enumerate(DIRECTIONS):
        index_rows = jnp.broadcast_to(out_rows[:, index_dir, :][:, None, :], (DOMAINS, LOADS, H))
        picked = jnp.take_along_axis(terms, index_rows, axis=2)
        used = (slot_ids[None, None, :] < out_counts[:, index_dir][:, None, None]).astype(jnp.float32)
        picked = picked * used
        grid = picked.reshape(N_DOM, N_SUB, LOADS, H)
        axis_pos = 0 if axis_name == "dom" else 1
        arrived = shifted(grid, axis_pos, offset).reshape(DOMAINS, LOADS, H)
        summed = jax.vmap(add_rows)(summed, in_rows[:, index_dir, :], arrived)
    return summed


def per_domain(field):
    return field.reshape(LOADS, DOMAINS, SUB_N).transpose(1, 0, 2)


def batch_dot(pair):
    return jnp.dot(pair[0], pair[1], preferred_element_type=jnp.float32)


def batch_dot_right(pair):
    return jnp.dot(pair[0], pair[1].T, preferred_element_type=jnp.float32)


def reference(rhs, start, stiffness, local_inverse, basis, weights, coarse_inverse, orders, out_rows, out_counts, in_rows):
    row_mask = (jnp.arange(SUB_N)[None, :] < orders[:, None]).astype(jnp.float32)[:, None, :]
    loads_rhs = per_domain(rhs)
    iterate = per_domain(start) * row_mask
    stiff_blocks = stiffness.reshape(DOMAINS, SUB_N, SUB_N)
    inverse_blocks = local_inverse.reshape(DOMAINS, SUB_N, SUB_N)
    basis_blocks = basis.reshape(NV, DOMAINS, SUB_N).transpose(1, 0, 2)
    weight_rows = weights.reshape(DOMAINS, 1, SUB_N)
    residual = loads_rhs
    for step in range(ITERS):
        iterate_bf = iterate.astype(jnp.bfloat16)
        product = lax.map(batch_dot, (iterate_bf, stiff_blocks))
        residual = row_mask * (loads_rhs - assemble(product, out_rows, out_counts, in_rows))
        residual_bf = residual.astype(jnp.bfloat16)
        local_fix = lax.map(batch_dot, (residual_bf, inverse_blocks))
        coarse_in = lax.map(batch_dot_right, (residual_bf, basis_blocks))
        coarse_all = coarse_in.transpose(1, 0, 2).reshape(LOADS, NC)
        coarse_out = lax.dot_general(coarse_all, coarse_inverse, (((1,), (1,)), ((), ())), precision=lax.Precision.HIGHEST, preferred_element_type=jnp.float32)
        coarse_bf = coarse_out.reshape(LOADS, DOMAINS, NV).transpose(1, 0, 2).astype(jnp.bfloat16)
        coarse_fix = lax.map(batch_dot, (coarse_bf, basis_blocks))
        correction = weight_rows * row_mask * (local_fix + coarse_fix)
        iterate = iterate + assemble(correction, out_rows, out_counts, in_rows)
    solution = iterate.transpose(1, 0, 2).reshape(LOADS, ROWS)
    residual_out = residual.transpose(1, 0, 2).reshape(LOADS, ROWS)
    return solution, residual_out
```

```python
import jax
import jax.numpy as jnp
from jax import lax
from jax.experimental import pallas as pl
from jax.experimental.pallas import tpu as pltpu
from jax.sharding import Mesh
from jax.sharding import PartitionSpec as P

Z, Y, C, X = 12, 8, 2, 4
PLANE = Y * C * X
N = 768
NV = 24
H = 128
EDGE = 256
F32, BF16 = jnp.float32, jnp.bfloat16
ALL = ("z", "y", "c", "x")
CHIPS = ("z", "y", "c")


def vmem(count):
    return [pl.BlockSpec(memory_space=pltpu.VMEM)] * count


def thirds(value):
    high = value.astype(BF16)
    rest = value - high.astype(F32)
    middle = rest.astype(BF16)
    low = (rest - middle.astype(F32)).astype(BF16)
    return jnp.concatenate([high, middle, low], axis=0)


def times_selection(value, selection):
    parts = jnp.dot(thirds(value), selection, preferred_element_type=F32)
    return parts[0:2] + parts[2:4] + parts[4:6]


def parities():
    chip = lax.axis_index("z") * Y + lax.axis_index("y")
    return lax.axis_index("x") % 2 == 0, chip % 2 == 0, lax.axis_index("c") == 0


def mask_of(orders_ref, width=N, first=0):
    return lax.broadcasted_iota(jnp.int32, (1, width), 1) + first < orders_ref[0, 0]


def send_messages(field, select, own_x, own_c, own_y):
    picked = times_selection(field, select)
    way = [picked[:, j * H : (j + 1) * H] for j in range(6)]
    even_x, even_chip, _ = parities()
    own_x[0] = jnp.where(even_x, way[0], way[1])
    own_x[1] = jnp.where(even_x, way[1], way[0])
    own_c[...] = picked[:, 2 * H : 4 * H]
    own_y[0] = jnp.where(even_chip, way[4], way[5])
    own_y[1] = jnp.where(even_chip, way[5], way[4])


def arrivals(xa, xb, pair, ya, yb):
    even_x, even_chip, first_core = parities()
    xa, xb, pair = xa[...], xb[...], pair[...]
    below = jnp.where(even_chip, yb[...], ya[...])
    above = jnp.where(even_chip, ya[...], yb[...])
    return jnp.concatenate(
        [
            jnp.where(even_x, xb, xa),
            jnp.where(even_x, xa, xb),
            jnp.where(first_core, below[:, H:], pair[:, :H]),
            jnp.where(first_core, pair[:, H:], above[:, H:]),
            below[:, :H],
            above[:, :H],
        ],
        axis=1,
    )


def first_kernel(start, stiff, orders, out_rows, counts, select, edge, own_x, own_c, own_y):
    rows = lax.broadcasted_iota(jnp.int32, (EDGE, H), 0)
    slots = lax.broadcasted_iota(jnp.int32, (1, H), 1)
    for j in range(6):
        listed = jnp.where(slots < counts[0, j], out_rows[0, j : j + 1, :], -1)
        select[:, j * H : (j + 1) * H] = (rows == listed).astype(F32).astype(BF16)
    iterate = jnp.where(mask_of(orders), start[...], 0.0)
    product = jnp.dot(iterate.astype(BF16), stiff[...], preferred_element_type=F32)
    edge[...] = product
    send_messages(product, select[...], own_x, own_c, own_y)


def rest_kernel(start, stiff_b, stiff_c, orders, in_rows, spread, rest):
    rows = lax.broadcasted_iota(jnp.int32, (EDGE, H), 0)
    for j in range(6):
        hit = (rows == in_rows[0, j : j + 1, :]).astype(F32)
        spread[j * H : (j + 1) * H, :] = hit.T.astype(BF16)
    iterate = jnp.where(mask_of(orders), start[...], 0.0).astype(BF16)
    rest[:, :EDGE] = jnp.dot(iterate, stiff_b[...], preferred_element_type=F32)
    rest[:, EDGE:] = jnp.dot(iterate, stiff_c[...], preferred_element_type=F32)


def residual_kernel(edge, rest, xa, xb, pair, ya, yb, spread, rhs, orders, basis, residual, rounded, rows):
    summed = edge[...] + times_selection(arrivals(xa, xb, pair, ya, yb), spread[...])
    total = jnp.concatenate([summed, rest[...]], axis=1)
    value = jnp.where(mask_of(orders), rhs[...] - total, 0.0)
    residual[...] = value
    low = value.astype(BF16)
    rounded[...] = low
    padded = jnp.concatenate([value, jnp.zeros((6, N), F32)], axis=0).astype(BF16)
    coarse = lax.dot_general(padded, basis[...], (((1,), (1,)), ((), ())), preferred_element_type=F32)
    place = lax.axis_index("y") * (C * X) + lax.axis_index("c") * X + lax.axis_index("x")
    shift = (24 * place) % 128
    turned = pltpu.roll(coarse, shift, 1)
    turned_far = pltpu.roll(turned, 64, 1)
    rows[...] = jnp.broadcast_to(turned[0:1] + turned_far[1:2], (PLANE, 128))


def repack_kernel(rows, out, packed):
    taken = rows[...]
    far = pltpu.roll(taken, 64, 1)
    place = lax.broadcasted_iota(jnp.int32, (PLANE, 128), 0)
    lane = lax.broadcasted_iota(jnp.int32, (PLANE, 128), 1)
    within = (lane - NV * place + NV * PLANE) & 127
    row = jnp.where(within < NV, (NV * (place & 15) + within) >> 7, -1)
    for load, field in enumerate((taken, far)):
        for r in range(3):
            kept = jnp.where(row == r, field, 0.0)
            for group in range(4):
                packed[load * 12 + group * 3 + r : load * 12 + group * 3 + r + 1, :] = jnp.sum(
                    kept[group * 16 : (group + 1) * 16], axis=0, keepdims=True
                )
    whole = packed[...]
    for z in range(Z):
        out[z] = whole


def local_kernel(rounded, inverse, local):
    local[...] = jnp.dot(rounded[...], inverse[...], preferred_element_type=F32)


def coarse_kernel(gathered, inverse, basis, weights, orders, local, select, correction, own_x, own_c, own_y):
    sums = [[jnp.zeros((NV, 128), F32) for _ in range(2)] for _ in range(2)]
    for t in range(Z * 12):
        z, r = divmod(t, 12)
        block = inverse[:, t * 128 : (t + 1) * 128]
        for load in range(2):
            sums[load][t % 2] += block * gathered[z, load * 12 + r : load * 12 + r + 1, :]
    vectors = basis[...].astype(F32)
    fixes = []
    for load in range(2):
        coarse = jnp.sum(sums[load][0] + sums[load][1], axis=1, keepdims=True)
        coarse = coarse.astype(BF16).astype(F32)
        fixes.append(jnp.sum(vectors * coarse, axis=0, keepdims=True))
    fix = jnp.concatenate(fixes, axis=0)
    value = jnp.where(mask_of(orders), weights[...] * (local[...] + fix), 0.0)
    correction[...] = value
    send_messages(value[:, :EDGE], select[...], own_x, own_c, own_y)


def last_kernel(start, orders, correction, xa, xb, pair, ya, yb, spread, solved):
    arrived = times_selection(arrivals(xa, xb, pair, ya, yb), spread[...])
    value = jnp.where(mask_of(orders), start[...], 0.0) + correction[...]
    solved[...] = value
    solved[:, :EDGE] = value[:, :EDGE] + arrived


def message_shapes():
    return [
        jax.ShapeDtypeStruct((2, 2, H), F32),
        jax.ShapeDtypeStruct((2, 2 * H), F32),
        jax.ShapeDtypeStruct((2, 2, H), F32),
    ]


def exchange(own_x, own_c, own_y):
    chips = Z * Y
    pairs_c = [(d, d ^ 1) for d in range(C)]
    even_x = [(d, d ^ 1) for d in range(X)]
    odd_x = [(1, 2), (2, 1)]
    even_chips = [(2 * q + c, 2 * (q ^ 1) + c) for q in range(chips) for c in range(C)]
    odd_chips = []
    for q in range(1, chips - 1, 2):
        for c in range(C):
            odd_chips += [(2 * q + c, 2 * q + 2 + c), (2 * q + 2 + c, 2 * q + c)]
    pair = lax.ppermute(own_c, "c", pairs_c)
    xa = lax.ppermute(own_x[0], "x", even_x)
    xb = lax.ppermute(own_x[1], "x", odd_x)
    even_chip = parities()[1]
    up, down = pair[:, :H], pair[:, H:]
    ya = jnp.concatenate([own_y[0], jnp.where(even_chip, up, down)], axis=1)
    yb = jnp.concatenate([own_y[1], jnp.where(even_chip, down, up)], axis=1)
    ya = lax.ppermute(ya, CHIPS, even_chips)
    yb = lax.ppermute(yb, CHIPS, odd_chips)
    return xa, xb, pair, ya, yb


def per_device(
    rhs, start, stiffness, local_inverse, basis, weights, coarse_inverse, orders, out_rows, out_counts, in_rows
):
    smem = pl.BlockSpec(memory_space=pltpu.SMEM)
    orders = orders.reshape(1, 1)
    whole = lambda shape: pl.BlockSpec(shape, lambda i: (0,) * len(shape))
    smem_grid = pl.BlockSpec(memory_space=pltpu.SMEM)
    select, edge, own_x, own_c, own_y = pl.pallas_call(
        first_kernel,
        grid=(1,),
        in_specs=[whole((2, N)), whole((N, EDGE)), smem_grid, whole((1, 6, H)), smem_grid],
        out_specs=[whole((EDGE, 6 * H)), whole((2, EDGE)), whole((2, 2, H)), whole((2, 2 * H)), whole((2, 2, H))],
        out_shape=[jax.ShapeDtypeStruct((EDGE, 6 * H), BF16), jax.ShapeDtypeStruct((2, EDGE), F32)]
        + message_shapes(),
    )(start, stiffness, orders, out_rows, out_counts)
    spread, rest = pl.pallas_call(
        rest_kernel,
        grid=(1,),
        in_specs=[
            whole((2, N)),
            pl.BlockSpec((N, EDGE), lambda i: (0, 1)),
            pl.BlockSpec((N, EDGE), lambda i: (0, 2)),
            smem_grid,
            whole((1, 6, H)),
        ],
        out_specs=[whole((6 * H, EDGE)), whole((2, 2 * EDGE))],
        out_shape=[jax.ShapeDtypeStruct((6 * H, EDGE), BF16), jax.ShapeDtypeStruct((2, 2 * EDGE), F32)],
    )(start, stiffness, stiffness, orders, in_rows)
    basis_rows = jnp.pad(basis, ((0, 128 - NV), (0, 0)))
    arrived = exchange(own_x, own_c, own_y)
    residual, rounded, rows = pl.pallas_call(
        residual_kernel,
        in_specs=vmem(9) + [smem] + vmem(1),
        out_specs=vmem(3),
        out_shape=[
            jax.ShapeDtypeStruct((2, N), F32),
            jax.ShapeDtypeStruct((2, N), BF16),
            jax.ShapeDtypeStruct((PLANE, 128), F32),
        ],
    )(edge, rest, *arrived, spread, rhs, orders, basis_rows)
    rows = lax.all_to_all(rows.reshape(PLANE, 1, 128), ("y", "c", "x"), 0, 0).reshape(PLANE, 128)
    local = pl.pallas_call(
        local_kernel,
        in_specs=vmem(2),
        out_specs=vmem(1)[0],
        out_shape=jax.ShapeDtypeStruct((2, N), F32),
    )(rounded, local_inverse)
    gathered = pl.pallas_call(
        repack_kernel,
        in_specs=vmem(1),
        out_specs=vmem(1)[0],
        out_shape=jax.ShapeDtypeStruct((Z, 2 * 12, 128), F32),
        scratch_shapes=[pltpu.VMEM((2 * 12, 128), F32)],
    )(rows)
    gathered = lax.all_to_all(gathered, "z", 0, 0)
    correction, own_x, own_c, own_y = pl.pallas_call(
        coarse_kernel,
        in_specs=vmem(4) + [smem] + vmem(2),
        out_specs=vmem(4),
        out_shape=[jax.ShapeDtypeStruct((2, N), F32)] + message_shapes(),
    )(gathered, coarse_inverse, basis, weights.reshape(1, N), orders, local, select)
    arrived = exchange(own_x, own_c, own_y)
    solved = pl.pallas_call(
        last_kernel,
        in_specs=vmem(1) + [smem] + vmem(7),
        out_specs=vmem(1)[0],
        out_shape=jax.ShapeDtypeStruct((2, N), F32),
    )(start, orders, correction, *arrived, spread)
    return solved, residual


def solution(mesh):
    fine = Mesh(mesh.devices.reshape(Z, Y, C, X), ALL)
    return jax.shard_map(
        per_device,
        mesh=fine,
        in_specs=(
            P(None, ALL),
            P(None, ALL),
            P(ALL, None),
            P(ALL, None),
            P(None, ALL),
            P(ALL),
            P(ALL, None),
            P(ALL),
            P(ALL, None, None),
            P(ALL, None),
            P(ALL, None, None),
        ),
        out_specs=(P(None, ALL), P(None, ALL)),
        check_vma=False,
    )
```

```python
import jax
import jax.numpy as jnp
from jax import lax
from jax.experimental import pallas as pl
from jax.experimental.pallas import tpu as pltpu
from jax.sharding import Mesh
from jax.sharding import PartitionSpec as P

Z, Y, C, X = 12, 8, 2, 4
PLANE = Y * C * X
N = 768
NV = 24
H = 128
EDGE = 256
F32, BF16 = jnp.float32, jnp.bfloat16
ALL = ("z", "y", "c", "x")
CHIPS = ("z", "y", "c")
LEAN = pltpu.CompilerParams(vmem_limit_bytes=8 << 20)


def on_chip(kernel, out_shape, args, scalars=(), far=(), scratch=()):
    def space(i):
        return pltpu.SMEM if i in scalars else pltpu.HBM if i in far else pltpu.VMEM

    specs = [pl.BlockSpec(memory_space=space(i)) for i in range(len(args))]
    args = [a if i in scalars else pltpu.with_memory_space_constraint(a, space(i)) for i, a in enumerate(args)]
    return pl.pallas_call(
        kernel,
        in_specs=specs,
        out_specs=[pl.BlockSpec(memory_space=pltpu.VMEM)] * len(out_shape),
        out_shape=[pltpu.VMEM(shape, dtype) for shape, dtype in out_shape],
        scratch_shapes=list(scratch),
        compiler_params=LEAN,
    )(*args)


def thirds(value):
    high = value.astype(BF16)
    rest = value - high.astype(F32)
    middle = rest.astype(BF16)
    low = (rest - middle.astype(F32)).astype(BF16)
    return jnp.concatenate([high, middle, low], axis=0)


def times_selection(value, selection):
    parts = jnp.dot(thirds(value), selection, preferred_element_type=F32)
    return parts[0:2] + parts[2:4] + parts[4:6]


def parities():
    chip = lax.axis_index("z") * Y + lax.axis_index("y")
    return lax.axis_index("x") % 2 == 0, chip % 2 == 0, lax.axis_index("c") == 0


def mask_of(orders_ref, width=N, first=0):
    return lax.broadcasted_iota(jnp.int32, (1, width), 1) + first < orders_ref[0, 0]


def send_messages(field, select, own_xa, own_xb, own_c, own_ya, own_yb):
    picked = times_selection(field, select)
    way = [picked[:, j * H : (j + 1) * H] for j in range(6)]
    even_x, even_chip, _ = parities()
    own_xa[...] = jnp.where(even_x, way[0], way[1])
    own_xb[...] = jnp.where(even_x, way[1], way[0])
    own_c[...] = picked[:, 2 * H : 4 * H]
    own_ya[...] = jnp.where(even_chip, way[4], way[5])
    own_yb[...] = jnp.where(even_chip, way[5], way[4])


def arrivals(xa, xb, pair, ya, yb):
    even_x, even_chip, first_core = parities()
    xa, xb, pair = xa[...], xb[...], pair[...]
    below = jnp.where(even_chip, yb[...], ya[...])
    above = jnp.where(even_chip, ya[...], yb[...])
    return jnp.concatenate(
        [
            jnp.where(even_x, xb, xa),
            jnp.where(even_x, xa, xb),
            jnp.where(first_core, below[:, H:], pair[:, :H]),
            jnp.where(first_core, pair[:, H:], above[:, H:]),
            below[:, :H],
            above[:, :H],
        ],
        axis=1,
    )


def first_kernel(start, stiff, orders, out_rows, counts, select, edge, own_xa, own_xb, own_c, own_ya, own_yb, columns, fields, listing, done):
    copies = [
        pltpu.make_async_copy(out_rows, listing, done.at[0]),
        pltpu.make_async_copy(start, fields, done.at[1]),
        pltpu.make_async_copy(stiff.at[:, pl.ds(0, EDGE)], columns, done.at[2]),
    ]
    for copy in copies:
        copy.start()
    copies[0].wait()
    rows = lax.broadcasted_iota(jnp.int32, (EDGE, H), 0)
    slots = lax.broadcasted_iota(jnp.int32, (1, H), 1)
    for j in range(6):
        listed = jnp.where(slots < counts[0, j], listing[j], -1)
        select[:, j * H : (j + 1) * H] = (rows == listed).astype(F32).astype(BF16)
    copies[1].wait()
    iterate = jnp.where(mask_of(orders), fields[...], 0.0).astype(BF16)
    copies[2].wait()
    product = jnp.dot(iterate, columns[...], preferred_element_type=F32)
    edge[...] = product
    send_messages(product, select[...], own_xa, own_xb, own_c, own_ya, own_yb)


def rest_kernel(start, stiff, orders, in_rows, spread, rest, columns, fields, listing, done):
    copies = [
        pltpu.make_async_copy(in_rows, listing, done.at[0]),
        pltpu.make_async_copy(start, fields, done.at[1]),
        pltpu.make_async_copy(stiff.at[:, pl.ds(EDGE, N - EDGE)], columns, done.at[2]),
    ]
    for copy in copies:
        copy.start()
    copies[0].wait()
    rows = lax.broadcasted_iota(jnp.int32, (EDGE, H), 0)
    for j in range(6):
        hit = (rows == listing[j]).astype(F32)
        spread[j * H : (j + 1) * H, :] = hit.T.astype(BF16)
    copies[1].wait()
    iterate = jnp.where(mask_of(orders), fields[...], 0.0).astype(BF16)
    copies[2].wait()
    rest[...] = jnp.dot(iterate, columns[...], preferred_element_type=F32)


def residual_kernel(edge, rest, xa, xb, pair, ya, yb, spread, rhs, orders, basis, inverse, _, residual, local, rows, held, done):
    copy = pltpu.make_async_copy(inverse, held, done)
    copy.start()
    summed = edge[...] + times_selection(arrivals(xa, xb, pair, ya, yb), spread[...])
    total = jnp.concatenate([summed, rest[...]], axis=1)
    value = jnp.where(mask_of(orders), rhs[...] - total, 0.0)
    residual[...] = value
    padded = jnp.concatenate([value, jnp.zeros((6, N), F32)], axis=0).astype(BF16)
    coarse = lax.dot_general(padded, basis[...], (((1,), (1,)), ((), ())), preferred_element_type=F32)
    coarse = jnp.concatenate([coarse, jnp.zeros((8, 128 - NV), F32)], axis=1)
    place = lax.axis_index("y") * (C * X) + lax.axis_index("c") * X + lax.axis_index("x")
    shift = (24 * place) % 128
    turned = pltpu.roll(coarse, shift, 1)
    turned_far = pltpu.roll(turned, 64, 1)
    rows[...] = jnp.broadcast_to(turned[0:1] + turned_far[1:2], (PLANE, 128))
    copy.wait()
    local[...] = jnp.dot(value.astype(BF16), held[...], preferred_element_type=F32)


def repack_kernel(rows, out, packed):
    taken = rows[...]
    far = pltpu.roll(taken, 64, 1)
    place = lax.broadcasted_iota(jnp.int32, (PLANE, 128), 0)
    lane = lax.broadcasted_iota(jnp.int32, (PLANE, 128), 1)
    within = (lane - NV * place + NV * PLANE) & 127
    row = jnp.where(within < NV, (NV * (place & 15) + within) >> 7, -1)
    for load, field in enumerate((taken, far)):
        for r in range(3):
            kept = jnp.where(row == r, field, 0.0)
            for group in range(4):
                packed[load * 12 + group * 3 + r : load * 12 + group * 3 + r + 1, :] = jnp.sum(
                    kept[group * 16 : (group + 1) * 16], axis=0, keepdims=True
                )
    whole = packed[...]
    for z in range(Z):
        out[z] = whole


def coarse_kernel(gathered, inverse, basis, weights, orders, local, select, correction, *own):
    sums = [[jnp.zeros((NV, 128), F32) for _ in range(2)] for _ in range(2)]
    for t in range(Z * 12):
        z, r = divmod(t, 12)
        block = inverse[:, t * 128 : (t + 1) * 128]
        for load in range(2):
            sums[load][t % 2] += block * gathered[z, load * 12 + r : load * 12 + r + 1, :]
    vectors = basis[...].astype(F32)
    fixes = []
    for load in range(2):
        coarse = jnp.sum(sums[load][0] + sums[load][1], axis=1, keepdims=True)
        coarse = coarse.astype(BF16).astype(F32)
        fixes.append(jnp.sum(vectors * coarse, axis=0, keepdims=True))
    fix = jnp.concatenate(fixes, axis=0)
    weight_row = jnp.concatenate([weights[j : j + 1, :] for j in range(6)], axis=1)
    value = jnp.where(mask_of(orders), weight_row * (local[...] + fix), 0.0)
    correction[...] = value
    send_messages(value[:, :EDGE], select[...], *own)


def last_kernel(start, orders, correction, xa, xb, pair, ya, yb, spread, solved):
    arrived = times_selection(arrivals(xa, xb, pair, ya, yb), spread[...])
    value = jnp.where(mask_of(orders), start[...], 0.0) + correction[...]
    solved[...] = value
    solved[:, :EDGE] = value[:, :EDGE] + arrived


MESSAGES = [((2, H), F32), ((2, H), F32), ((2, 2 * H), F32), ((2, H), F32), ((2, H), F32)]


def exchange(own_xa, own_xb, own_c, own_ya, own_yb):
    chips = Z * Y
    pairs_c = [(d, d ^ 1) for d in range(C)]
    even_x = [(d, d ^ 1) for d in range(X)]
    odd_x = [(1, 2), (2, 1)]
    even_chips = [(2 * q + c, 2 * (q ^ 1) + c) for q in range(chips) for c in range(C)]
    odd_chips = []
    for q in range(1, chips - 1, 2):
        for c in range(C):
            odd_chips += [(2 * q + c, 2 * q + 2 + c), (2 * q + 2 + c, 2 * q + c)]
    pair = lax.ppermute(own_c, "c", pairs_c)
    xa = lax.ppermute(own_xa, "x", even_x)
    xb = lax.ppermute(own_xb, "x", odd_x)
    even_chip = parities()[1]
    up, down = pair[:, :H], pair[:, H:]
    ya = jnp.concatenate([own_ya, jnp.where(even_chip, up, down)], axis=1)
    yb = jnp.concatenate([own_yb, jnp.where(even_chip, down, up)], axis=1)
    ya = lax.ppermute(ya, CHIPS, even_chips)
    yb = lax.ppermute(yb, CHIPS, odd_chips)
    return xa, xb, pair, ya, yb


def per_device(
    rhs, start, stiffness, local_inverse, basis, weights, coarse_inverse, orders, out_rows, out_counts, in_rows
):
    orders = orders.reshape(1, 1)
    out_rows = out_rows.reshape(6, 1, H)
    in_rows = in_rows.reshape(6, 1, H)
    arriving = [pltpu.VMEM((2, N), F32), pltpu.VMEM((6, 1, H), jnp.int32), pltpu.SemaphoreType.DMA((3,))]
    select, edge, *own = on_chip(
        first_kernel,
        [((EDGE, 6 * H), BF16), ((2, EDGE), F32)] + MESSAGES,
        [start, stiffness, orders, out_rows, out_counts],
        scalars=(2, 4),
        far=(0, 1, 3),
        scratch=[pltpu.VMEM((N, EDGE), BF16)] + arriving,
    )
    spread, rest = on_chip(
        rest_kernel,
        [((6 * H, EDGE), BF16), ((2, N - EDGE), F32)],
        [start, stiffness, orders, in_rows],
        scalars=(2,),
        far=(0, 1, 3),
        scratch=[pltpu.VMEM((N, N - EDGE), BF16)] + arriving,
    )
    arrived = exchange(*own)
    residual, local, rows = on_chip(
        residual_kernel,
        [((2, N), F32), ((2, N), F32), ((PLANE, 128), F32)],
        [edge, rest, *arrived, spread, rhs, orders, basis, local_inverse, coarse_inverse],
        scalars=(9,),
        far=(11,),
        scratch=[pltpu.VMEM((N, N), BF16), pltpu.SemaphoreType.DMA],
    )
    rows = lax.all_to_all(rows.reshape(PLANE, 1, 128), ("y", "c", "x"), 0, 0).reshape(PLANE, 128)
    (gathered,) = on_chip(
        repack_kernel, [((Z, 2 * 12, 128), F32)], [rows], scratch=[pltpu.VMEM((2 * 12, 128), F32)]
    )
    gathered = lax.all_to_all(gathered, "z", 0, 0)
    correction, *own = on_chip(
        coarse_kernel,
        [((2, N), F32)] + MESSAGES,
        [gathered, coarse_inverse, basis, weights.reshape(6, 128), orders, local, select],
        scalars=(4,),
    )
    arrived = exchange(*own)
    (solved,) = on_chip(last_kernel, [((2, N), F32)], [start, orders, correction, *arrived, spread], scalars=(1,))
    return solved, residual


def solution(mesh):
    fine = Mesh(mesh.devices.reshape(Z, Y, C, X), ALL)
    return jax.shard_map(
        per_device,
        mesh=fine,
        in_specs=(
            P(None, ALL),
            P(None, ALL),
            P(ALL, None),
            P(ALL, None),
            P(None, ALL),
            P(ALL),
            P(ALL, None),
            P(ALL),
            P(ALL, None, None),
            P(ALL, None),
            P(ALL, None, None),
        ),
        out_specs=(P(None, ALL), P(None, ALL)),
        check_vma=False,
    )
```

```python
import jax
import jax.numpy as jnp
from jax import lax
from jax.experimental import pallas as pl
from jax.experimental.pallas import tpu as pltpu
from jax.sharding import Mesh
from jax.sharding import PartitionSpec as P

Z, Y, C, X = 12, 8, 2, 4
PLANE = Y * C * X
N = 768
NV = 24
H = 128
EDGE = 256
F32, BF16 = jnp.float32, jnp.bfloat16
ALL = ("z", "y", "c", "x")
CHIPS = ("z", "y", "c")
LEAN = pltpu.CompilerParams(vmem_limit_bytes=8 << 20)


def on_chip(kernel, out_shape, args, far=(), scratch=(), scalars=()):
    spaces = [pltpu.SMEM if i in scalars else pltpu.HBM if i in far else pltpu.VMEM for i in range(len(args))]
    args = [a if i in scalars else pltpu.with_memory_space_constraint(a, spaces[i]) for i, a in enumerate(args)]
    return pl.pallas_call(
        kernel,
        in_specs=[pl.BlockSpec(memory_space=space) for space in spaces],
        out_specs=[pl.BlockSpec(memory_space=pltpu.VMEM)] * len(out_shape),
        out_shape=[pltpu.VMEM(shape, dtype) for shape, dtype in out_shape],
        scratch_shapes=list(scratch),
        compiler_params=LEAN,
    )(*args)


def thirds(value):
    high = value.astype(BF16)
    rest = value - high.astype(F32)
    middle = rest.astype(BF16)
    low = (rest - middle.astype(F32)).astype(BF16)
    return jnp.concatenate([high, middle, low], axis=0)


def times_selection(value, selection):
    parts = jnp.dot(thirds(value), selection, preferred_element_type=F32)
    return parts[0:2] + parts[2:4] + parts[4:6]


def write_slots(field, select, own):
    picked = times_selection(field, select)
    for j in range(6):
        own[j] = picked[:, j * H : (j + 1) * H]


def arrivals(both, moved):
    first = lax.axis_index("c") == 0
    up, down = 0, 5
    return jnp.concatenate(
        [
            jnp.where(first, moved[up + 3], moved[up + 4]),
            jnp.where(first, moved[down + 3], moved[down + 4]),
            jnp.where(first, moved[up + 2], both[2]),
            jnp.where(first, both[6 + 3], moved[down + 2]),
            jnp.where(first, moved[up], moved[up + 1]),
            jnp.where(first, moved[down], moved[down + 1]),
        ],
        axis=1,
    )


def exchange(own):
    chips = Z * Y
    both = lax.all_gather(own, "c", axis=0, tiled=True)
    first = lax.axis_index("c") == 0
    along_x = jnp.where(first, jnp.stack([both[0], both[6]]), jnp.stack([both[1], both[7]]))
    along_y = jnp.where(first, jnp.stack([both[4], both[10], both[8]]), jnp.stack([both[5], both[11], both[3]]))
    route_y = [(2 * q, 2 * q + 2) for q in range(chips - 1)] + [(2 * q + 1, 2 * q - 1) for q in range(1, chips)]
    route_x = [(d, d + 1) for d in range(X - 1)] + [(X + d, X + d - 1) for d in range(1, X)]
    got_y = lax.ppermute(along_y, CHIPS, route_y)
    got_x = lax.ppermute(along_x, ("c", "x"), route_x)
    moved = lax.all_gather(jnp.concatenate([got_y, got_x]), "c", axis=0, tiled=True)
    return both, moved


def first_kernel(start, stiff, orders, out_rows, counts, select, edge, mask, iterate, own, columns, fields, listing, count, done):
    copies = [
        pltpu.make_async_copy(counts, count, done.at[0]),
        pltpu.make_async_copy(out_rows, listing, done.at[1]),
        pltpu.make_async_copy(start, fields, done.at[2]),
        pltpu.make_async_copy(stiff.at[:, pl.ds(0, EDGE)], columns, done.at[3]),
    ]
    for copy in copies:
        copy.start()
    rows = lax.broadcasted_iota(jnp.int32, (EDGE, H), 0)
    slots = lax.broadcasted_iota(jnp.int32, (1, H), 1)
    copies[0].wait()
    copies[1].wait()
    for j in range(6):
        listed = jnp.where(slots < count[0, j], listing[j], -1)
        select[:, j * H : (j + 1) * H] = (rows == listed).astype(F32).astype(BF16)
    kept = lax.broadcasted_iota(jnp.int32, (1, N), 1) < orders[0]
    mask[...] = kept.astype(F32)
    copies[2].wait()
    masked = jnp.where(kept, fields[...], 0.0)
    iterate[...] = masked
    copies[3].wait()
    product = jnp.dot(masked.astype(BF16), columns[...], preferred_element_type=F32)
    edge[...] = product
    write_slots(product, select[...], own)


def rest_kernel(iterate, stiff, in_rows, inverse, spread, rest, held, columns, listing, done):
    copies = [
        pltpu.make_async_copy(in_rows, listing, done.at[0]),
        pltpu.make_async_copy(stiff.at[:, pl.ds(EDGE, N - EDGE)], columns, done.at[1]),
        pltpu.make_async_copy(inverse, held, done.at[2]),
    ]
    for copy in copies:
        copy.start()
    rows = lax.broadcasted_iota(jnp.int32, (EDGE, H), 0)
    copies[0].wait()
    for j in range(6):
        hit = (rows == listing[j]).astype(F32)
        spread[j * H : (j + 1) * H, :] = hit.T.astype(BF16)
    copies[1].wait()
    rest[...] = jnp.dot(iterate[...].astype(BF16), columns[...], preferred_element_type=F32)
    copies[2].wait()


def residual_kernel(edge, rest, both, moved, spread, rhs, mask, basis, _, residual, rounded, rows):
    summed = edge[...] + times_selection(arrivals(both, moved), spread[...])
    total = jnp.concatenate([summed, rest[...]], axis=1)
    value = jnp.where(mask[...] > 0.0, rhs[...] - total, 0.0)
    residual[...] = value
    rounded[...] = value.astype(BF16)
    padded = jnp.concatenate([value, jnp.zeros((6, N), F32)], axis=0).astype(BF16)
    coarse = lax.dot_general(padded, basis[...], (((1,), (1,)), ((), ())), preferred_element_type=F32)
    coarse = jnp.concatenate([coarse, jnp.zeros((8, 128 - NV), F32)], axis=1)
    place = lax.axis_index("y") * (C * X) + lax.axis_index("c") * X + lax.axis_index("x")
    shift = (24 * place) % 128
    turned = pltpu.roll(coarse, shift, 1)
    turned_far = pltpu.roll(turned, 64, 1)
    rows[...] = jnp.broadcast_to(turned[0:1] + turned_far[1:2], (PLANE, 128))


def repack_kernel(rows, out, packed):
    taken = rows[...]
    far = pltpu.roll(taken, 64, 1)
    place = lax.broadcasted_iota(jnp.int32, (PLANE, 128), 0)
    lane = lax.broadcasted_iota(jnp.int32, (PLANE, 128), 1)
    within = (lane - NV * place + NV * PLANE) & 127
    row = jnp.where(within < NV, (NV * (place & 15) + within) >> 7, -1)
    for load, field in enumerate((taken, far)):
        for r in range(3):
            kept = jnp.where(row == r, field, 0.0)
            for group in range(4):
                packed[load * 12 + group * 3 + r : load * 12 + group * 3 + r + 1, :] = jnp.sum(
                    kept[group * 16 : (group + 1) * 16], axis=0, keepdims=True
                )
    whole = packed[...]
    for z in range(Z):
        out[z] = whole


def coarse_kernel(gathered, inverse, basis, weights, mask, rounded, held, select, correction, own):
    sums = [[jnp.zeros((NV, 128), F32) for _ in range(2)] for _ in range(2)]
    for t in range(Z * 12):
        z, r = divmod(t, 12)
        block = inverse[:, t * 128 : (t + 1) * 128]
        for load in range(2):
            sums[load][t % 2] += block * gathered[z, load * 12 + r : load * 12 + r + 1, :]
    vectors = basis[...].astype(F32)
    fixes = []
    for load in range(2):
        coarse = jnp.sum(sums[load][0] + sums[load][1], axis=1, keepdims=True)
        coarse = coarse.astype(BF16).astype(F32)
        fixes.append(jnp.sum(vectors * coarse, axis=0, keepdims=True))
    fix = jnp.concatenate(fixes, axis=0)
    local = jnp.dot(rounded[...], held[...], preferred_element_type=F32)
    weight_row = jnp.concatenate([weights[j : j + 1, :] for j in range(6)], axis=1)
    value = weight_row * mask[...] * (local + fix)
    correction[...] = value
    write_slots(value[:, :EDGE], select[...], own)


def last_kernel(iterate, correction, both, moved, spread, solved):
    arrived = times_selection(arrivals(both, moved), spread[...])
    value = iterate[...] + correction[...]
    solved[...] = value
    solved[:, :EDGE] = value[:, :EDGE] + arrived


def per_device(
    rhs, start, stiffness, local_inverse, basis, weights, coarse_inverse, orders, out_rows, out_counts, in_rows
):
    out_rows = out_rows.reshape(6, 1, H)
    in_rows = in_rows.reshape(6, 1, H)
    slots = ((6, 2, H), F32)
    listing = pltpu.VMEM((6, 1, H), jnp.int32)
    select, edge, mask, iterate, own = on_chip(
        first_kernel,
        [((EDGE, 6 * H), BF16), ((2, EDGE), F32), ((1, N), F32), ((2, N), F32), slots],
        [start, stiffness, orders, out_rows, out_counts],
        far=(0, 1, 3, 4),
        scalars=(2,),
        scratch=[
            pltpu.VMEM((N, EDGE), BF16),
            pltpu.VMEM((2, N), F32),
            listing,
            pltpu.SMEM((1, 6), jnp.int32),
            pltpu.SemaphoreType.DMA((4,)),
        ],
    )
    spread, rest, held = on_chip(
        rest_kernel,
        [((6 * H, EDGE), BF16), ((2, N - EDGE), F32), ((N, N), BF16)],
        [iterate, stiffness, in_rows, local_inverse],
        far=(1, 2, 3),
        scratch=[pltpu.VMEM((N, N - EDGE), BF16), listing, pltpu.SemaphoreType.DMA((3,))],
    )
    both, moved = exchange(own)
    residual, rounded, rows = on_chip(
        residual_kernel,
        [((2, N), F32), ((2, N), BF16), ((PLANE, 128), F32)],
        [edge, rest, both, moved, spread, rhs, mask, basis, coarse_inverse],
    )
    rows = lax.all_to_all(rows.reshape(PLANE, 1, 128), ("y", "c", "x"), 0, 0).reshape(PLANE, 128)
    (gathered,) = on_chip(
        repack_kernel, [((Z, 2 * 12, 128), F32)], [rows], scratch=[pltpu.VMEM((2 * 12, 128), F32)]
    )
    gathered = lax.all_to_all(gathered, "z", 0, 0)
    correction, own = on_chip(
        coarse_kernel,
        [((2, N), F32), slots],
        [gathered, coarse_inverse, basis, weights.reshape(6, 128), mask, rounded, held, select],
    )
    both, moved = exchange(own)
    (solved,) = on_chip(last_kernel, [((2, N), F32)], [iterate, correction, both, moved, spread])
    return solved, residual


def solution(mesh):
    fine = Mesh(mesh.devices.reshape(Z, Y, C, X), ALL)
    return jax.shard_map(
        per_device,
        mesh=fine,
        in_specs=(
            P(None, ALL),
            P(None, ALL),
            P(ALL, None),
            P(ALL, None),
            P(None, ALL),
            P(ALL),
            P(ALL, None),
            P(ALL),
            P(ALL, None, None),
            P(ALL, None),
            P(ALL, None, None),
        ),
        out_specs=(P(None, ALL), P(None, ALL)),
        check_vma=False,
    )
```

```python
import jax
import jax.numpy as jnp
from jax import lax
from jax.experimental import pallas as pl
from jax.experimental.pallas import tpu as pltpu
from jax.sharding import Mesh
from jax.sharding import PartitionSpec as P

Z, Y, C, X = 12, 8, 2, 4
PLANE = Y * C * X
N = 768
NV = 24
H = 128
EDGE = 256
F32, BF16 = jnp.float32, jnp.bfloat16
ALL = ("z", "y", "c", "x")
CHIPS = ("z", "y", "c")
LEAN = pltpu.CompilerParams(vmem_limit_bytes=8 << 20)


def on_chip(kernel, out_shape, args, far=(), scratch=(), loose=()):
    spaces = [pl.ANY if i in loose else pltpu.HBM if i in far else pltpu.VMEM for i in range(len(args))]
    args = [a if i in loose else pltpu.with_memory_space_constraint(a, spaces[i]) for i, a in enumerate(args)]
    return pl.pallas_call(
        kernel,
        in_specs=[pl.BlockSpec(memory_space=space) for space in spaces],
        out_specs=[pl.BlockSpec(memory_space=pltpu.VMEM)] * len(out_shape),
        out_shape=[pltpu.VMEM(shape, dtype) for shape, dtype in out_shape],
        scratch_shapes=list(scratch),
        compiler_params=LEAN,
    )(*args)


def thirds(value):
    high = value.astype(BF16)
    rest = value - high.astype(F32)
    middle = rest.astype(BF16)
    low = (rest - middle.astype(F32)).astype(BF16)
    return jnp.concatenate([high, middle, low], axis=0)


def times_selection(value, selection):
    parts = jnp.dot(thirds(value), selection, preferred_element_type=F32)
    return parts[0:2] + parts[2:4] + parts[4:6]


def write_slots(field, select, own):
    picked = times_selection(field, select)
    for j in range(6):
        own[j] = picked[:, j * H : (j + 1) * H]


def arrivals(both, moved):
    first = lax.axis_index("c") == 0
    up, down = 0, 5
    return jnp.concatenate(
        [
            jnp.where(first, moved[up + 3], moved[up + 4]),
            jnp.where(first, moved[down + 3], moved[down + 4]),
            jnp.where(first, moved[up + 2], both[2]),
            jnp.where(first, both[6 + 3], moved[down + 2]),
            jnp.where(first, moved[up], moved[up + 1]),
            jnp.where(first, moved[down], moved[down + 1]),
        ],
        axis=1,
    )


def exchange(own):
    chips = Z * Y
    both = lax.all_gather(own, "c", axis=0, tiled=True)
    first = lax.axis_index("c") == 0
    along_x = jnp.where(first, jnp.stack([both[0], both[6]]), jnp.stack([both[1], both[7]]))
    along_y = jnp.where(first, jnp.stack([both[4], both[10], both[8]]), jnp.stack([both[5], both[11], both[3]]))
    route_y = [(2 * q, 2 * q + 2) for q in range(chips - 1)] + [(2 * q + 1, 2 * q - 1) for q in range(1, chips)]
    route_x = [(d, d + 1) for d in range(X - 1)] + [(X + d, X + d - 1) for d in range(1, X)]
    got_y = lax.ppermute(along_y, CHIPS, route_y)
    got_x = lax.ppermute(along_x, ("c", "x"), route_x)
    moved = lax.all_gather(jnp.concatenate([got_y, got_x]), "c", axis=0, tiled=True)
    return both, moved


def first_kernel(
    start, stiff, orders, out_rows, counts, in_rows, select, edge, mask, iterate, own, beyond, arriving, columns, fields, listing, order, count, done
):
    copies = [
        pltpu.make_async_copy(counts, count, done.at[0]),
        pltpu.make_async_copy(out_rows, listing, done.at[1]),
        pltpu.make_async_copy(orders, order, done.at[2]),
        pltpu.make_async_copy(start, fields, done.at[3]),
        pltpu.make_async_copy(stiff.at[:, pl.ds(0, EDGE)], columns, done.at[4]),
        pltpu.make_async_copy(in_rows, arriving, done.at[5]),
        pltpu.make_async_copy(stiff.at[:, pl.ds(EDGE, N - EDGE)], beyond, done.at[6]),
    ]
    for copy in copies:
        copy.start()
    rows = lax.broadcasted_iota(jnp.int32, (EDGE, H), 0)
    slots = lax.broadcasted_iota(jnp.int32, (1, H), 1)
    copies[0].wait()
    copies[1].wait()
    for j in range(6):
        listed = jnp.where(slots < count[0, j], listing[j], -1)
        select[:, j * H : (j + 1) * H] = (rows == listed).astype(F32).astype(BF16)
    copies[2].wait()
    kept = lax.broadcasted_iota(jnp.int32, (1, N), 1) < order[0]
    mask[...] = kept.astype(F32)
    copies[3].wait()
    masked = jnp.where(kept, fields[...], 0.0)
    iterate[...] = masked
    copies[4].wait()
    product = jnp.dot(masked.astype(BF16), columns[...], preferred_element_type=F32)
    edge[...] = product
    write_slots(product, select[...], own)
    copies[5].wait()
    copies[6].wait()


def rest_kernel(iterate, beyond, arriving, spread, rest):
    rows = lax.broadcasted_iota(jnp.int32, (EDGE, H), 0)
    for j in range(6):
        hit = (rows == arriving[j]).astype(F32)
        spread[j * H : (j + 1) * H, :] = hit.T.astype(BF16)
    rest[...] = jnp.dot(iterate[...].astype(BF16), beyond[...], preferred_element_type=F32)


def residual_kernel(edge, rest, both, moved, spread, rhs, mask, basis, _, residual, rounded, rows):
    summed = edge[...] + times_selection(arrivals(both, moved), spread[...])
    total = jnp.concatenate([summed, rest[...]], axis=1)
    value = jnp.where(mask[...] > 0.0, rhs[...] - total, 0.0)
    residual[...] = value
    rounded[...] = value.astype(BF16)
    padded = jnp.concatenate([value, jnp.zeros((6, N), F32)], axis=0).astype(BF16)
    coarse = lax.dot_general(padded, basis[...], (((1,), (1,)), ((), ())), preferred_element_type=F32)
    coarse = jnp.concatenate([coarse, jnp.zeros((8, 128 - NV), F32)], axis=1)
    place = lax.axis_index("y") * (C * X) + lax.axis_index("c") * X + lax.axis_index("x")
    shift = (24 * place) % 128
    turned = pltpu.roll(coarse, shift, 1)
    turned_far = pltpu.roll(turned, 64, 1)
    rows[...] = jnp.broadcast_to(turned[0:1] + turned_far[1:2], (PLANE, 128))


def repack_kernel(rows, out, packed):
    taken = rows[...]
    far = pltpu.roll(taken, 64, 1)
    place = lax.broadcasted_iota(jnp.int32, (PLANE, 128), 0)
    lane = lax.broadcasted_iota(jnp.int32, (PLANE, 128), 1)
    within = (lane - NV * place + NV * PLANE) & 127
    row = jnp.where(within < NV, (NV * (place & 15) + within) >> 7, -1)
    for load, field in enumerate((taken, far)):
        for r in range(3):
            kept = jnp.where(row == r, field, 0.0)
            for group in range(4):
                packed[load * 12 + group * 3 + r : load * 12 + group * 3 + r + 1, :] = jnp.sum(
                    kept[group * 16 : (group + 1) * 16], axis=0, keepdims=True
                )
    whole = packed[...]
    for z in range(Z):
        out[z] = whole


def coarse_kernel(gathered, inverse, basis, weights, mask, rounded, held, select, correction, own):
    sums = [[jnp.zeros((NV, 128), F32) for _ in range(2)] for _ in range(2)]
    for t in range(Z * 12):
        z, r = divmod(t, 12)
        block = inverse[:, t * 128 : (t + 1) * 128]
        for load in range(2):
            sums[load][t % 2] += block * gathered[z, load * 12 + r : load * 12 + r + 1, :]
    vectors = basis[...].astype(F32)
    fixes = []
    for load in range(2):
        coarse = jnp.sum(sums[load][0] + sums[load][1], axis=1, keepdims=True)
        coarse = coarse.astype(BF16).astype(F32)
        fixes.append(jnp.sum(vectors * coarse, axis=0, keepdims=True))
    fix = jnp.concatenate(fixes, axis=0)
    local = jnp.dot(rounded[...], held[...], preferred_element_type=F32)
    weight_row = jnp.concatenate([weights[j : j + 1, :] for j in range(6)], axis=1)
    value = weight_row * mask[...] * (local + fix)
    correction[...] = value
    write_slots(value[:, :EDGE], select[...], own)


def last_kernel(iterate, correction, both, moved, spread, solved):
    arrived = times_selection(arrivals(both, moved), spread[...])
    value = iterate[...] + correction[...]
    solved[...] = value
    solved[:, :EDGE] = value[:, :EDGE] + arrived


def per_device(
    rhs, start, stiffness, local_inverse, basis, weights, coarse_inverse, orders, out_rows, out_counts, in_rows
):
    out_rows = out_rows.reshape(6, 1, H)
    in_rows = in_rows.reshape(6, 1, H)
    slots = ((6, 2, H), F32)
    select, edge, mask, iterate, own, beyond, arriving = on_chip(
        first_kernel,
        [
            ((EDGE, 6 * H), BF16),
            ((2, EDGE), F32),
            ((1, N), F32),
            ((2, N), F32),
            slots,
            ((N, N - EDGE), BF16),
            ((6, 1, H), jnp.int32),
        ],
        [start, stiffness, orders, out_rows, out_counts, in_rows],
        far=(0, 1, 3, 4, 5),
        loose=(2,),
        scratch=[
            pltpu.VMEM((N, EDGE), BF16),
            pltpu.VMEM((2, N), F32),
            pltpu.VMEM((6, 1, H), jnp.int32),
            pltpu.SMEM((1,), jnp.int32),
            pltpu.SMEM((1, 6), jnp.int32),
            pltpu.SemaphoreType.DMA((7,)),
        ],
    )
    coarse_inverse, own = lax.optimization_barrier((coarse_inverse, own))
    spread, rest = on_chip(
        rest_kernel, [((6 * H, EDGE), BF16), ((2, N - EDGE), F32)], [iterate, beyond, arriving]
    )
    both, moved = exchange(own)
    residual, rounded, rows = on_chip(
        residual_kernel,
        [((2, N), F32), ((2, N), BF16), ((PLANE, 128), F32)],
        [edge, rest, both, moved, spread, rhs, mask, basis, coarse_inverse],
    )
    rows = lax.all_to_all(rows.reshape(PLANE, 1, 128), ("y", "c", "x"), 0, 0).reshape(PLANE, 128)
    (gathered,) = on_chip(
        repack_kernel, [((Z, 2 * 12, 128), F32)], [rows], scratch=[pltpu.VMEM((2 * 12, 128), F32)]
    )
    gathered = lax.all_to_all(gathered, "z", 0, 0)
    correction, own = on_chip(
        coarse_kernel,
        [((2, N), F32), slots],
        [gathered, coarse_inverse, basis, weights.reshape(6, 128), mask, rounded, local_inverse, select],
    )
    both, moved = exchange(own)
    (solved,) = on_chip(last_kernel, [((2, N), F32)], [iterate, correction, both, moved, spread])
    return solved, residual


def solution(mesh):
    fine = Mesh(mesh.devices.reshape(Z, Y, C, X), ALL)
    return jax.shard_map(
        per_device,
        mesh=fine,
        in_specs=(
            P(None, ALL),
            P(None, ALL),
            P(ALL, None),
            P(ALL, None),
            P(None, ALL),
            P(ALL),
            P(ALL, None),
            P(ALL),
            P(ALL, None, None),
            P(ALL, None),
            P(ALL, None, None),
        ),
        out_specs=(P(None, ALL), P(None, ALL)),
        check_vma=False,
    )
```

```python
import jax
import jax.numpy as jnp
from jax import lax
from jax.experimental import pallas as pl
from jax.experimental.pallas import tpu as pltpu
from jax.sharding import Mesh
from jax.sharding import PartitionSpec as P

Z, Y, C, X = 12, 8, 2, 4
LAYER = Y * X
HALF = Z * LAYER * 24
N = 768
NV = 24
H = 128
EDGE = 256
F32, BF16 = jnp.float32, jnp.bfloat16
ALL = ("z", "y", "c", "x")
CHIPS = ("z", "y", "c")
LEAN = pltpu.CompilerParams(vmem_limit_bytes=8 << 20)


def on_chip(kernel, out_shape, args, far=(), scratch=(), loose=()):
    spaces = [pl.ANY if i in loose else pltpu.HBM if i in far else pltpu.VMEM for i in range(len(args))]
    args = [a if i in loose else pltpu.with_memory_space_constraint(a, spaces[i]) for i, a in enumerate(args)]
    return pl.pallas_call(
        kernel,
        in_specs=[pl.BlockSpec(memory_space=space) for space in spaces],
        out_specs=[pl.BlockSpec(memory_space=pltpu.VMEM)] * len(out_shape),
        out_shape=[pltpu.VMEM(shape, dtype) for shape, dtype in out_shape],
        scratch_shapes=list(scratch),
        compiler_params=LEAN,
    )(*args)


def thirds(value):
    high = value.astype(BF16)
    rest = value - high.astype(F32)
    middle = rest.astype(BF16)
    low = (rest - middle.astype(F32)).astype(BF16)
    return jnp.concatenate([high, middle, low], axis=0)


def times_selection(value, selection):
    parts = jnp.dot(thirds(value), selection, preferred_element_type=F32)
    return parts[0:2] + parts[2:4] + parts[4:6]


def selection_of(listed):
    rows = lax.broadcasted_iota(jnp.int32, (EDGE, H), 0)
    return [(rows == one).astype(F32).astype(BF16) for one in listed]


def spread_of(arriving):
    rows = lax.broadcasted_iota(jnp.int32, (EDGE, H), 0)
    return jnp.concatenate([(rows == arriving[j]).astype(F32).T.astype(BF16) for j in range(6)], axis=0)


def arrivals(both, moved):
    first = lax.axis_index("c") == 0
    up, down, second = 0, moved.shape[0] // 2, both.shape[0] // 2
    return jnp.concatenate(
        [
            jnp.where(first, moved[up + 3], moved[up + 4]),
            jnp.where(first, moved[down + 3], moved[down + 4]),
            jnp.where(first, moved[up + 2], both[2]),
            jnp.where(first, both[second + 3], moved[down + 2]),
            jnp.where(first, moved[up], moved[up + 1]),
            jnp.where(first, moved[down], moved[down + 1]),
        ],
        axis=1,
    )


def across(both):
    chips = Z * Y
    first = lax.axis_index("c") == 0
    own, other = both[: both.shape[0] // 2], both[both.shape[0] // 2 :]
    along_x = jnp.where(first, jnp.stack([own[0], other[0]]), jnp.stack([own[1], other[1]]))
    along_y = jnp.where(first, jnp.stack([own[4], other[4], other[2]]), jnp.stack([own[5], other[5], own[3]]))
    route_y = [(2 * q, 2 * q + 2) for q in range(chips - 1)] + [(2 * q + 1, 2 * q - 1) for q in range(1, chips)]
    route_x = [(d, d + 1) for d in range(X - 1)] + [(X + d, X + d - 1) for d in range(1, X)]
    got_y = lax.ppermute(along_y, CHIPS, route_y)
    got_x = lax.ppermute(along_x, ("c", "x"), route_x)
    return [got_y, got_x]


def in_pair(value):
    return lax.all_gather(value, "c", axis=0, tiled=True)


def first_kernel(
    start, stiff, orders, out_rows, counts, in_rows, inverse, edge, mask, iterate, own, beyond, arriving, near, columns, fields, listing, order, count, done
):
    copies = [
        pltpu.make_async_copy(counts, count, done.at[0]),
        pltpu.make_async_copy(out_rows, listing, done.at[1]),
        pltpu.make_async_copy(orders, order, done.at[2]),
        pltpu.make_async_copy(start, fields, done.at[3]),
        pltpu.make_async_copy(stiff.at[:, pl.ds(0, EDGE)], columns, done.at[4]),
        pltpu.make_async_copy(in_rows, arriving, done.at[5]),
        pltpu.make_async_copy(stiff.at[:, pl.ds(EDGE, N - EDGE)], beyond, done.at[6]),
        pltpu.make_async_copy(inverse, near, done.at[7]),
    ]
    for copy in copies:
        copy.start()
    slots = lax.broadcasted_iota(jnp.int32, (1, H), 1)
    copies[0].wait()
    copies[1].wait()
    listed = [jnp.where(slots < count[0, j], listing[j], -1) for j in range(6)]
    select = selection_of(listed)
    for j in range(6):
        own[6 + j // 2, j % 2 : j % 2 + 1, :] = listed[j].astype(F32)
    copies[2].wait()
    kept = lax.broadcasted_iota(jnp.int32, (1, N), 1) < order[0]
    mask[...] = kept.astype(F32)
    copies[3].wait()
    masked = jnp.where(kept, fields[...], 0.0)
    iterate[...] = masked
    copies[4].wait()
    product = jnp.dot(masked.astype(BF16), columns[...], preferred_element_type=F32)
    edge[...] = product
    picked = times_selection(product, jnp.concatenate(select, axis=1))
    for j in range(6):
        own[j] = picked[:, j * H : (j + 1) * H]
    copies[5].wait()
    copies[6].wait()
    copies[7].wait()


def weight_row(weights):
    return jnp.concatenate([weights[j : j + 1, :] for j in range(6)], axis=1)


def rest_kernel(iterate, beyond, mask, weights, basis, inverse, rest, edges, mine, theirs):
    first = lax.axis_index("c") == 0
    rest[...] = jnp.dot(iterate[...].astype(BF16), beyond[...], preferred_element_type=F32)
    weighted = basis[...].astype(F32) * (weight_row(weights) * mask[...])
    for half in range(2):
        for row in range(0, NV, 2):
            edges[half * 12 + row // 2] = weighted[row : row + 2, half * H : (half + 1) * H]
    for group in range(HALF // 384):
        block = inverse[:, group * 768 : (group + 1) * 768]
        low = jnp.concatenate([block[:, k * 192 : k * 192 + 96] for k in range(4)], axis=1)
        high = jnp.concatenate([block[:, k * 192 + 96 : k * 192 + 192] for k in range(4)], axis=1)
        mine[:, group * 384 : (group + 1) * 384] = jnp.where(first, low, high)
        theirs[:, group * 384 : (group + 1) * 384] = jnp.where(first, high, low)


def residual_kernel(edge, rest, both, moved, arriving, rhs, mask, basis, residual, rounded, rows):
    summed = edge[...] + times_selection(arrivals(both, moved), spread_of(arriving))
    total = jnp.concatenate([summed, rest[...]], axis=1)
    value = jnp.where(mask[...] > 0.0, rhs[...] - total, 0.0)
    residual[...] = value
    rounded[...] = value.astype(BF16)
    padded = jnp.concatenate([value, jnp.zeros((6, N), F32)], axis=0).astype(BF16)
    coarse = lax.dot_general(padded, basis[...], (((1,), (1,)), ((), ())), preferred_element_type=F32)
    coarse = jnp.concatenate([coarse, jnp.zeros((8, 128 - NV), F32)], axis=1)
    place = lax.axis_index("y") * X + lax.axis_index("x")
    shift = (24 * place) % 128
    turned = pltpu.roll(coarse, shift, 1)
    turned_far = pltpu.roll(turned, 64, 1)
    rows[...] = jnp.broadcast_to(turned[0:1] + turned_far[1:2], (LAYER, 128))


def repack_kernel(rows, out, packed):
    taken = rows[...]
    far = pltpu.roll(taken, 64, 1)
    place = lax.broadcasted_iota(jnp.int32, (LAYER, 128), 0)
    lane = lax.broadcasted_iota(jnp.int32, (LAYER, 128), 1)
    within = (lane - NV * place + NV * LAYER) & 127
    row = jnp.where(within < NV, (NV * (place & 15) + within) >> 7, -1)
    for load, field in enumerate((taken, far)):
        for r in range(3):
            kept = jnp.where(row == r, field, 0.0)
            for group in range(2):
                packed[load * 6 + group * 3 + r : load * 6 + group * 3 + r + 1, :] = jnp.sum(
                    kept[group * 16 : (group + 1) * 16], axis=0, keepdims=True
                )
    whole = packed[...]
    for z in range(Z):
        out[z] = whole


def partial_kernel(gathered, mine, given, rounded, held, weights, mask, shared, local):
    first = lax.axis_index("c") == 0
    sums = [[[jnp.zeros((NV, 128), F32) for _ in range(2)] for _ in range(2)] for _ in range(2)]
    for t in range(HALF // 128):
        z, r = divmod(t, 6)
        blocks = [rows[:, t * 128 : (t + 1) * 128] for rows in (mine, given)]
        for load in range(2):
            factor = gathered[z, load * 6 + r : load * 6 + r + 1, :]
            for owner in range(2):
                sums[owner][load][t % 2] += blocks[owner] * factor
    lane = lax.broadcasted_iota(jnp.int32, (NV, 128), 1)
    tile = jnp.zeros((NV, 128), F32)
    for owner in range(2):
        at = jnp.where(first, 2 * owner, 2 - 2 * owner)
        for load in range(2):
            part = jnp.sum(sums[owner][load][0] + sums[owner][load][1], axis=1, keepdims=True)
            tile = jnp.where(lane == at + load, part, tile)
    shared[:NV] = tile
    weighted = weight_row(weights) * mask[...] * jnp.dot(rounded[...], held[...], preferred_element_type=F32)
    local[...] = weighted
    for load in range(2):
        for half in range(2):
            at = NV + 2 * load + half
            shared[at : at + 1, :] = weighted[load : load + 1, half * H : (half + 1) * H]
    shared[NV + 4 :] = jnp.zeros((4, 128), F32)


def coarse_kernel(shared, local, basis, weights, mask, moved, before, correction, both):
    first = lax.axis_index("c") == 0
    total = shared[:NV] + shared[32 : 32 + NV]
    total = total.astype(BF16).astype(F32)
    vectors = basis[...].astype(F32)
    partner_local = jnp.where(first, shared[56:60], shared[24:28])
    fixes, partner = [], []
    for load in range(2):
        pair = [total[:, load : load + 1], total[:, 2 + load : 3 + load]]
        coarse = jnp.where(first, pair[0], pair[1])
        fixes.append(jnp.sum(vectors * coarse, axis=0, keepdims=True))
        coarse = jnp.where(first, pair[1], pair[0])
        halves = []
        for half in range(2):
            terms = jnp.zeros((2, H), F32)
            for row in range(0, NV, 2):
                at = 5 + half * 12 + row // 2
                terms += jnp.where(first, moved[5 + NV + at], moved[at]) * coarse[row : row + 2]
            halves.append(partner_local[2 * load + half : 2 * load + half + 1, :] + jnp.sum(terms, axis=0, keepdims=True))
        partner.append(jnp.concatenate(halves, axis=1))
    value = local[...] + weight_row(weights) * mask[...] * jnp.concatenate(fixes, axis=0)
    correction[...] = value
    low = [before[6 + j // 2, j % 2 : j % 2 + 1, :].astype(jnp.int32) for j in range(6)]
    high = [before[15 + j // 2, j % 2 : j % 2 + 1, :].astype(jnp.int32) for j in range(6)]
    select = selection_of([jnp.where(first, low[j], high[j]) for j in range(6)])
    partner_select = selection_of([jnp.where(first, high[j], low[j]) for j in range(6)])
    own = times_selection(value[:, :EDGE], jnp.concatenate(select, axis=1))
    other = times_selection(jnp.concatenate(partner, axis=0), jnp.concatenate(partner_select, axis=1))
    for j in range(6):
        mine, theirs = own[:, j * H : (j + 1) * H], other[:, j * H : (j + 1) * H]
        both[j] = jnp.where(first, mine, theirs)
        both[6 + j] = jnp.where(first, theirs, mine)


def last_kernel(iterate, correction, both, moved, arriving, solved):
    arrived = times_selection(arrivals(both, moved), spread_of(arriving))
    value = iterate[...] + correction[...]
    solved[...] = value
    solved[:, :EDGE] = value[:, :EDGE] + arrived


def per_device(
    rhs, start, stiffness, local_inverse, basis, weights, coarse_inverse, orders, out_rows, out_counts, in_rows
):
    out_rows = out_rows.reshape(6, 1, H)
    in_rows = in_rows.reshape(6, 1, H)
    weights = weights.reshape(6, 128)
    edge, mask, iterate, own, beyond, arriving, near = on_chip(
        first_kernel,
        [
            ((2, EDGE), F32),
            ((1, N), F32),
            ((2, N), F32),
            ((9, 2, H), F32),
            ((N, N - EDGE), BF16),
            ((6, 1, H), jnp.int32),
            ((NV, C * HALF), F32),
        ],
        [start, stiffness, orders, out_rows, out_counts, in_rows, coarse_inverse],
        far=(0, 1, 3, 4, 5, 6),
        loose=(2,),
        scratch=[
            pltpu.VMEM((N, EDGE), BF16),
            pltpu.VMEM((2, N), F32),
            pltpu.VMEM((6, 1, H), jnp.int32),
            pltpu.SMEM((1,), jnp.int32),
            pltpu.SMEM((1, 6), jnp.int32),
            pltpu.SemaphoreType.DMA((8,)),
        ],
    )
    both = in_pair(own)
    going = across(both)
    rest, edges, mine, theirs = on_chip(
        rest_kernel,
        [((2, N - EDGE), F32), ((NV, 2, H), F32), ((NV, HALF), F32), ((NV, HALF), F32)],
        [iterate, beyond, mask, weights, basis, near],
    )
    given = lax.ppermute(theirs, "c", [(0, 1), (1, 0)])
    before = both
    moved = in_pair(jnp.concatenate(going + [edges]))
    edges = moved
    residual, rounded, rows = on_chip(
        residual_kernel,
        [((2, N), F32), ((2, N), BF16), ((LAYER, 128), F32)],
        [edge, rest, both, moved, arriving, rhs, mask, basis],
    )
    rows = lax.all_to_all(rows.reshape(LAYER, 1, 128), ("y", "x"), 0, 0).reshape(LAYER, 128)
    (gathered,) = on_chip(repack_kernel, [((Z, 12, 128), F32)], [rows], scratch=[pltpu.VMEM((12, 128), F32)])
    gathered = lax.all_to_all(gathered, "z", 0, 0)
    shared, local = on_chip(
        partial_kernel,
        [((32, 128), F32), ((2, N), F32)],
        [gathered, mine, given, rounded, local_inverse, weights, mask],
    )
    correction, both = on_chip(
        coarse_kernel,
        [((2, N), F32), ((12, 2, H), F32)],
        [in_pair(shared), local, basis, weights, mask, edges, before],
    )
    moved = in_pair(jnp.concatenate(across(both)))
    (solved,) = on_chip(last_kernel, [((2, N), F32)], [iterate, correction, both, moved, arriving])
    return solved, residual


def solution(mesh):
    fine = Mesh(mesh.devices.reshape(Z, Y, C, X), ALL)
    return jax.shard_map(
        per_device,
        mesh=fine,
        in_specs=(
            P(None, ALL),
            P(None, ALL),
            P(ALL, None),
            P(ALL, None),
            P(None, ALL),
            P(ALL),
            P(ALL, None),
            P(ALL),
            P(ALL, None, None),
            P(ALL, None),
            P(ALL, None, None),
        ),
        out_specs=(P(None, ALL), P(None, ALL)),
        check_vma=False,
    )
```

```python
import jax
import jax.numpy as jnp
from jax import lax
from jax.experimental import pallas as pl
from jax.experimental.pallas import tpu as pltpu
from jax.sharding import Mesh
from jax.sharding import PartitionSpec as P

Z, Y, C, X = 12, 8, 2, 4
LAYER = Y * X
HALF = Z * LAYER * 24
N = 768
NV = 24
H = 128
EDGE = 256
F32, BF16 = jnp.float32, jnp.bfloat16
ALL = ("z", "y", "c", "x")
CHIPS = ("z", "y", "c")
LEAN = pltpu.CompilerParams(vmem_limit_bytes=8 << 20)


def on_chip(kernel, out_shape, args, far=(), scratch=(), loose=(), work=None):
    spaces = [pl.ANY if i in loose else pltpu.HBM if i in far else pltpu.VMEM for i in range(len(args))]
    args = [a if i in loose else pltpu.with_memory_space_constraint(a, spaces[i]) for i, a in enumerate(args)]
    return pl.pallas_call(
        kernel,
        in_specs=[pl.BlockSpec(memory_space=space) for space in spaces],
        out_specs=[pl.BlockSpec(memory_space=pltpu.VMEM)] * len(out_shape),
        out_shape=[pltpu.VMEM(shape, dtype) for shape, dtype in out_shape],
        scratch_shapes=list(scratch),
        compiler_params=LEAN,
        cost_estimate=work,
    )(*args)


def thirds(value):
    high = value.astype(BF16)
    rest = value - high.astype(F32)
    middle = rest.astype(BF16)
    low = (rest - middle.astype(F32)).astype(BF16)
    return jnp.concatenate([high, middle, low], axis=0)


def times_selection(value, selection):
    parts = jnp.dot(thirds(value), selection, preferred_element_type=F32)
    return parts[0:2] + parts[2:4] + parts[4:6]


def selection_of(listed):
    rows = lax.broadcasted_iota(jnp.int32, (EDGE, H), 0)
    return [(rows == one).astype(F32).astype(BF16) for one in listed]


def spread_of(arriving):
    rows = lax.broadcasted_iota(jnp.int32, (EDGE, H), 0)
    return jnp.concatenate([(rows == arriving[j]).astype(F32).T.astype(BF16) for j in range(6)], axis=0)


def arrivals(both, moved):
    first = lax.axis_index("c") == 0
    up, down, second = 0, moved.shape[0] // 2, both.shape[0] // 2
    return jnp.concatenate(
        [
            jnp.where(first, moved[up + 3], moved[up + 4]),
            jnp.where(first, moved[down + 3], moved[down + 4]),
            jnp.where(first, moved[up + 2], both[2]),
            jnp.where(first, both[second + 3], moved[down + 2]),
            jnp.where(first, moved[up], moved[up + 1]),
            jnp.where(first, moved[down], moved[down + 1]),
        ],
        axis=1,
    )


def across(both):
    chips = Z * Y
    first = lax.axis_index("c") == 0
    own, other = both[: both.shape[0] // 2], both[both.shape[0] // 2 :]
    along_x = jnp.where(first, jnp.stack([own[0], other[0]]), jnp.stack([own[1], other[1]]))
    along_y = jnp.where(first, jnp.stack([own[4], other[4], other[2]]), jnp.stack([own[5], other[5], own[3]]))
    route_y = [(2 * q, 2 * q + 2) for q in range(chips - 1)] + [(2 * q + 1, 2 * q - 1) for q in range(1, chips)]
    route_x = [(d, d + 1) for d in range(X - 1)] + [(X + d, X + d - 1) for d in range(1, X)]
    got_y = lax.ppermute(along_y, CHIPS, route_y)
    got_x = lax.ppermute(along_x, ("c", "x"), route_x)
    return [got_y, got_x]


def in_pair(value):
    return lax.all_gather(value, "c", axis=0, tiled=True)


def first_kernel(
    start, stiff, orders, out_rows, counts, in_rows, edge, mask, iterate, own, beyond, arriving, columns, fields, listing, order, count, done
):
    copies = [
        pltpu.make_async_copy(counts, count, done.at[0]),
        pltpu.make_async_copy(out_rows, listing, done.at[1]),
        pltpu.make_async_copy(orders, order, done.at[2]),
        pltpu.make_async_copy(start, fields, done.at[3]),
        pltpu.make_async_copy(stiff.at[:, pl.ds(0, EDGE)], columns, done.at[4]),
        pltpu.make_async_copy(in_rows, arriving, done.at[5]),
        pltpu.make_async_copy(stiff.at[:, pl.ds(EDGE, N - EDGE)], beyond, done.at[6]),
    ]
    for copy in copies:
        copy.start()
    slots = lax.broadcasted_iota(jnp.int32, (1, H), 1)
    copies[0].wait()
    copies[1].wait()
    listed = [jnp.where(slots < count[0, j], listing[j], -1) for j in range(6)]
    select = selection_of(listed)
    for j in range(6):
        own[6 + j // 2, j % 2 : j % 2 + 1, :] = listed[j].astype(F32)
    copies[2].wait()
    kept = lax.broadcasted_iota(jnp.int32, (1, N), 1) < order[0]
    mask[...] = kept.astype(F32)
    copies[3].wait()
    masked = jnp.where(kept, fields[...], 0.0)
    iterate[...] = masked
    copies[4].wait()
    product = jnp.dot(masked.astype(BF16), columns[...], preferred_element_type=F32)
    edge[...] = product
    picked = times_selection(product, jnp.concatenate(select, axis=1))
    for j in range(6):
        own[j] = picked[:, j * H : (j + 1) * H]
    copies[5].wait()
    copies[6].wait()


def weight_row(weights):
    return jnp.concatenate([weights[j : j + 1, :] for j in range(6)], axis=1)


def rest_kernel(iterate, beyond, mask, weights, basis, inverse, arriving, spread, rest, edges, mine, theirs):
    first = lax.axis_index("c") == 0
    spread[...] = spread_of(arriving)
    rest[...] = jnp.dot(iterate[...].astype(BF16), beyond[...], preferred_element_type=F32)
    weighted = basis[...].astype(F32) * (weight_row(weights) * mask[...])
    for half in range(2):
        for row in range(0, NV, 2):
            edges[half * 12 + row // 2] = weighted[row : row + 2, half * H : (half + 1) * H]
    for group in range(HALF // 384):
        block = inverse[:, group * 768 : (group + 1) * 768]
        low = jnp.concatenate([block[:, k * 192 : k * 192 + 96] for k in range(4)], axis=1)
        high = jnp.concatenate([block[:, k * 192 + 96 : k * 192 + 192] for k in range(4)], axis=1)
        mine[:, group * 384 : (group + 1) * 384] = jnp.where(first, low, high)
        theirs[:, group * 384 : (group + 1) * 384] = jnp.where(first, high, low)


def residual_kernel(edge, rest, both, moved, spread, rhs, mask, basis, residual, rounded, rows):
    summed = edge[...] + times_selection(arrivals(both, moved), spread[...])
    total = jnp.concatenate([summed, rest[...]], axis=1)
    value = jnp.where(mask[...] > 0.0, rhs[...] - total, 0.0)
    residual[...] = value
    rounded[...] = value.astype(BF16)
    padded = jnp.concatenate([value, jnp.zeros((6, N), F32)], axis=0).astype(BF16)
    coarse = lax.dot_general(padded, basis[...], (((1,), (1,)), ((), ())), preferred_element_type=F32)
    coarse = jnp.concatenate([coarse, jnp.zeros((8, 128 - NV), F32)], axis=1)
    place = lax.axis_index("y") * X + lax.axis_index("x")
    shift = (24 * place) % 128
    turned = pltpu.roll(coarse, shift, 1)
    turned_far = pltpu.roll(turned, 64, 1)
    rows[...] = jnp.broadcast_to(turned[0:1] + turned_far[1:2], (LAYER, 128))


def repack_kernel(rows, out, packed):
    taken = rows[...]
    far = pltpu.roll(taken, 64, 1)
    place = lax.broadcasted_iota(jnp.int32, (LAYER, 128), 0)
    lane = lax.broadcasted_iota(jnp.int32, (LAYER, 128), 1)
    within = (lane - NV * place + NV * LAYER) & 127
    row = jnp.where(within < NV, (NV * (place & 15) + within) >> 7, -1)
    for load, field in enumerate((taken, far)):
        for r in range(3):
            kept = jnp.where(row == r, field, 0.0)
            for group in range(2):
                packed[load * 6 + group * 3 + r : load * 6 + group * 3 + r + 1, :] = jnp.sum(
                    kept[group * 16 : (group + 1) * 16], axis=0, keepdims=True
                )
    whole = packed[...]
    for z in range(Z):
        out[z] = whole


def partial_kernel(gathered, mine, given, rounded, held, weights, mask, shared, local):
    first = lax.axis_index("c") == 0
    sums = [[[jnp.zeros((NV, 128), F32) for _ in range(2)] for _ in range(2)] for _ in range(2)]
    for t in range(HALF // 128):
        z, r = divmod(t, 6)
        blocks = [rows[:, t * 128 : (t + 1) * 128] for rows in (mine, given)]
        for load in range(2):
            factor = gathered[z, load * 6 + r : load * 6 + r + 1, :]
            for owner in range(2):
                sums[owner][load][t % 2] += blocks[owner] * factor
    lane = lax.broadcasted_iota(jnp.int32, (NV, 128), 1)
    tile = jnp.zeros((NV, 128), F32)
    for owner in range(2):
        at = jnp.where(first, 2 * owner, 2 - 2 * owner)
        for load in range(2):
            part = jnp.sum(sums[owner][load][0] + sums[owner][load][1], axis=1, keepdims=True)
            tile = jnp.where(lane == at + load, part, tile)
    shared[:NV] = tile
    weighted = weight_row(weights) * mask[...] * jnp.dot(rounded[...], held[...], preferred_element_type=F32)
    local[...] = weighted
    for load in range(2):
        for half in range(2):
            at = NV + 2 * load + half
            shared[at : at + 1, :] = weighted[load : load + 1, half * H : (half + 1) * H]
    shared[NV + 4 :] = jnp.zeros((4, 128), F32)


def coarse_kernel(shared, local, basis, weights, mask, moved, before, correction, both):
    first = lax.axis_index("c") == 0
    total = shared[:NV] + shared[32 : 32 + NV]
    total = total.astype(BF16).astype(F32)
    vectors = basis[...].astype(F32)
    partner_local = jnp.where(first, shared[56:60], shared[24:28])
    fixes, partner = [], []
    for load in range(2):
        pair = [total[:, load : load + 1], total[:, 2 + load : 3 + load]]
        coarse = jnp.where(first, pair[0], pair[1])
        fixes.append(jnp.sum(vectors * coarse, axis=0, keepdims=True))
        coarse = jnp.where(first, pair[1], pair[0])
        halves = []
        for half in range(2):
            terms = jnp.zeros((2, H), F32)
            for row in range(0, NV, 2):
                at = 5 + half * 12 + row // 2
                terms += jnp.where(first, moved[5 + NV + at], moved[at]) * coarse[row : row + 2]
            halves.append(partner_local[2 * load + half : 2 * load + half + 1, :] + jnp.sum(terms, axis=0, keepdims=True))
        partner.append(jnp.concatenate(halves, axis=1))
    value = local[...] + weight_row(weights) * mask[...] * jnp.concatenate(fixes, axis=0)
    correction[...] = value
    low = [before[6 + j // 2, j % 2 : j % 2 + 1, :].astype(jnp.int32) for j in range(6)]
    high = [before[15 + j // 2, j % 2 : j % 2 + 1, :].astype(jnp.int32) for j in range(6)]
    select = selection_of([jnp.where(first, low[j], high[j]) for j in range(6)])
    partner_select = selection_of([jnp.where(first, high[j], low[j]) for j in range(6)])
    own = times_selection(value[:, :EDGE], jnp.concatenate(select, axis=1))
    other = times_selection(jnp.concatenate(partner, axis=0), jnp.concatenate(partner_select, axis=1))
    for j in range(6):
        mine, theirs = own[:, j * H : (j + 1) * H], other[:, j * H : (j + 1) * H]
        both[j] = jnp.where(first, mine, theirs)
        both[6 + j] = jnp.where(first, theirs, mine)


def last_kernel(iterate, correction, both, moved, spread, solved):
    arrived = times_selection(arrivals(both, moved), spread[...])
    value = iterate[...] + correction[...]
    solved[...] = value
    solved[:, :EDGE] = value[:, :EDGE] + arrived


def per_device(
    rhs, start, stiffness, local_inverse, basis, weights, coarse_inverse, orders, out_rows, out_counts, in_rows
):
    out_rows = out_rows.reshape(6, 1, H)
    in_rows = in_rows.reshape(6, 1, H)
    weights = weights.reshape(6, 128)
    edge, mask, iterate, own, beyond, arriving = on_chip(
        first_kernel,
        [
            ((2, EDGE), F32),
            ((1, N), F32),
            ((2, N), F32),
            ((9, 2, H), F32),
            ((N, N - EDGE), BF16),
            ((6, 1, H), jnp.int32),
        ],
        [start, stiffness, orders, out_rows, out_counts, in_rows],
        far=(0, 1, 3, 4, 5),
        work=pl.CostEstimate(flops=2 * 10**9, transcendentals=0, bytes_accessed=1 << 21),
        loose=(2,),
        scratch=[
            pltpu.VMEM((N, EDGE), BF16),
            pltpu.VMEM((2, N), F32),
            pltpu.VMEM((6, 1, H), jnp.int32),
            pltpu.SMEM((1,), jnp.int32),
            pltpu.SMEM((1, 6), jnp.int32),
            pltpu.SemaphoreType.DMA((7,)),
        ],
    )
    both = in_pair(own)
    going = across(both)
    spread, rest, edges, mine, theirs = on_chip(
        rest_kernel,
        [((6 * H, EDGE), BF16), ((2, N - EDGE), F32), ((NV, 2, H), F32), ((NV, HALF), F32), ((NV, HALF), F32)],
        [iterate, beyond, mask, weights, basis, coarse_inverse, arriving],
    )
    given = lax.ppermute(theirs, "c", [(0, 1), (1, 0)])
    before = both
    moved = in_pair(jnp.concatenate(going + [edges]))
    edges = moved
    residual, rounded, rows = on_chip(
        residual_kernel,
        [((2, N), F32), ((2, N), BF16), ((LAYER, 128), F32)],
        [edge, rest, both, moved, spread, rhs, mask, basis],
    )
    rows = lax.all_to_all(rows.reshape(LAYER, 1, 128), ("y", "x"), 0, 0).reshape(LAYER, 128)
    (gathered,) = on_chip(repack_kernel, [((Z, 12, 128), F32)], [rows], scratch=[pltpu.VMEM((12, 128), F32)])
    gathered = lax.all_to_all(gathered, "z", 0, 0)
    shared, local = on_chip(
        partial_kernel,
        [((32, 128), F32), ((2, N), F32)],
        [gathered, mine, given, rounded, local_inverse, weights, mask],
    )
    correction, both = on_chip(
        coarse_kernel,
        [((2, N), F32), ((12, 2, H), F32)],
        [in_pair(shared), local, basis, weights, mask, edges, before],
    )
    moved = in_pair(jnp.concatenate(across(both)))
    (solved,) = on_chip(last_kernel, [((2, N), F32)], [iterate, correction, both, moved, spread])
    return solved, residual


def solution(mesh):
    fine = Mesh(mesh.devices.reshape(Z, Y, C, X), ALL)
    return jax.shard_map(
        per_device,
        mesh=fine,
        in_specs=(
            P(None, ALL),
            P(None, ALL),
            P(ALL, None),
            P(ALL, None),
            P(None, ALL),
            P(ALL),
            P(ALL, None),
            P(ALL),
            P(ALL, None, None),
            P(ALL, None),
            P(ALL, None, None),
        ),
        out_specs=(P(None, ALL), P(None, ALL)),
        check_vma=False,
    )
```

```python
import jax
import jax.numpy as jnp
from jax import lax
from jax.experimental import pallas as pl
from jax.experimental.pallas import tpu as pltpu
from jax.sharding import Mesh
from jax.sharding import PartitionSpec as P

Z, Y, C, X = 12, 8, 2, 4
LAYER = Y * X
HALF = Z * LAYER * 24
N = 768
NV = 24
H = 128
EDGE = 256
F32, BF16 = jnp.float32, jnp.bfloat16
ALL = ("z", "y", "c", "x")
CHIPS = ("z", "y", "c")
LEAN = pltpu.CompilerParams(vmem_limit_bytes=8 << 20)


def on_chip(kernel, out_shape, args, far=(), scratch=(), loose=(), work=None):
    spaces = [pl.ANY if i in loose else pltpu.HBM if i in far else pltpu.VMEM for i in range(len(args))]
    args = [a if i in loose else pltpu.with_memory_space_constraint(a, spaces[i]) for i, a in enumerate(args)]
    return pl.pallas_call(
        kernel,
        in_specs=[pl.BlockSpec(memory_space=space) for space in spaces],
        out_specs=[pl.BlockSpec(memory_space=pltpu.VMEM)] * len(out_shape),
        out_shape=[pltpu.VMEM(shape, dtype) for shape, dtype in out_shape],
        scratch_shapes=list(scratch),
        compiler_params=LEAN,
        cost_estimate=work,
    )(*args)


def thirds(value):
    high = value.astype(BF16)
    rest = value - high.astype(F32)
    middle = rest.astype(BF16)
    low = (rest - middle.astype(F32)).astype(BF16)
    return jnp.concatenate([high, middle, low], axis=0)


def times_selection(value, selection):
    parts = jnp.dot(thirds(value), selection, preferred_element_type=F32)
    return parts[0:2] + parts[2:4] + parts[4:6]


def selection_of(listed):
    rows = lax.broadcasted_iota(jnp.int32, (EDGE, H), 0)
    return [(rows == one).astype(F32).astype(BF16) for one in listed]


def spread_of(arriving):
    rows = lax.broadcasted_iota(jnp.int32, (EDGE, H), 0)
    return jnp.concatenate([(rows == arriving[j]).astype(F32).T.astype(BF16) for j in range(6)], axis=0)


def arrivals(both, moved):
    first = lax.axis_index("c") == 0
    up, down, second = 0, moved.shape[0] // 2, both.shape[0] // 2
    return jnp.concatenate(
        [
            jnp.where(first, moved[up + 3], moved[up + 4]),
            jnp.where(first, moved[down + 3], moved[down + 4]),
            jnp.where(first, moved[up + 2], both[2]),
            jnp.where(first, both[second + 3], moved[down + 2]),
            jnp.where(first, moved[up], moved[up + 1]),
            jnp.where(first, moved[down], moved[down + 1]),
        ],
        axis=1,
    )


def across(both):
    chips = Z * Y
    first = lax.axis_index("c") == 0
    own, other = both[: both.shape[0] // 2], both[both.shape[0] // 2 :]
    along_x = jnp.where(first, jnp.stack([own[0], other[0]]), jnp.stack([own[1], other[1]]))
    along_y = jnp.where(first, jnp.stack([own[4], other[4], other[2]]), jnp.stack([own[5], other[5], own[3]]))
    route_y = [(2 * q, 2 * q + 2) for q in range(chips - 1)] + [(2 * q + 1, 2 * q - 1) for q in range(1, chips)]
    route_x = [(d, d + 1) for d in range(X - 1)] + [(X + d, X + d - 1) for d in range(1, X)]
    got_y = lax.ppermute(along_y, CHIPS, route_y)
    got_x = lax.ppermute(along_x, ("c", "x"), route_x)
    return [got_y, got_x]


def in_pair(value):
    return lax.all_gather(value, "c", axis=0, tiled=True)


def first_kernel(
    start, stiff, orders, out_rows, counts, in_rows, edge, mask, iterate, own, beyond, arriving, columns, fields, listing, order, count, done
):
    copies = [
        pltpu.make_async_copy(counts, count, done.at[0]),
        pltpu.make_async_copy(out_rows, listing, done.at[1]),
        pltpu.make_async_copy(orders, order, done.at[2]),
        pltpu.make_async_copy(start, fields, done.at[3]),
        pltpu.make_async_copy(stiff.at[:, pl.ds(0, EDGE)], columns, done.at[4]),
        pltpu.make_async_copy(in_rows, arriving, done.at[5]),
        pltpu.make_async_copy(stiff.at[:, pl.ds(EDGE, N - EDGE)], beyond, done.at[6]),
    ]
    for copy in copies:
        copy.start()
    slots = lax.broadcasted_iota(jnp.int32, (1, H), 1)
    copies[0].wait()
    copies[1].wait()
    listed = [jnp.where(slots < count[0, j], listing[j], -1) for j in range(6)]
    select = selection_of(listed)
    for j in range(6):
        own[6 + j // 2, j % 2 : j % 2 + 1, :] = listed[j].astype(F32)
    copies[2].wait()
    kept = lax.broadcasted_iota(jnp.int32, (1, N), 1) < order[0]
    mask[...] = kept.astype(F32)
    copies[3].wait()
    masked = jnp.where(kept, fields[...], 0.0)
    iterate[...] = masked
    copies[4].wait()
    product = jnp.dot(masked.astype(BF16), columns[...], preferred_element_type=F32)
    edge[...] = product
    picked = times_selection(product, jnp.concatenate(select, axis=1))
    for j in range(6):
        own[j] = picked[:, j * H : (j + 1) * H]
    copies[5].wait()
    copies[6].wait()


def weight_row(weights):
    return jnp.concatenate([weights[j : j + 1, :] for j in range(6)], axis=1)


def rest_kernel(iterate, beyond, mask, weights, basis, inverse, arriving, spread, rest, mine, theirs):
    first = lax.axis_index("c") == 0
    spread[...] = spread_of(arriving)
    rest[...] = jnp.dot(iterate[...].astype(BF16), beyond[...], preferred_element_type=F32)
    weighted = basis[...].astype(F32) * (weight_row(weights) * mask[...])
    theirs[:, HALF:] = weighted[:, :EDGE]
    for group in range(HALF // 384):
        block = inverse[:, group * 768 : (group + 1) * 768]
        low = jnp.concatenate([block[:, k * 192 : k * 192 + 96] for k in range(4)], axis=1)
        high = jnp.concatenate([block[:, k * 192 + 96 : k * 192 + 192] for k in range(4)], axis=1)
        mine[:, group * 384 : (group + 1) * 384] = jnp.where(first, low, high)
        theirs[:, group * 384 : (group + 1) * 384] = jnp.where(first, high, low)


def residual_kernel(edge, rest, both, moved, spread, rhs, mask, basis, residual, rounded, rows):
    summed = edge[...] + times_selection(arrivals(both, moved), spread[...])
    total = jnp.concatenate([summed, rest[...]], axis=1)
    value = jnp.where(mask[...] > 0.0, rhs[...] - total, 0.0)
    residual[...] = value
    rounded[...] = value.astype(BF16)
    padded = jnp.concatenate([value, jnp.zeros((6, N), F32)], axis=0).astype(BF16)
    coarse = lax.dot_general(padded, basis[...], (((1,), (1,)), ((), ())), preferred_element_type=F32)
    coarse = jnp.concatenate([coarse, jnp.zeros((8, 128 - NV), F32)], axis=1)
    place = lax.axis_index("y") * X + lax.axis_index("x")
    shift = (24 * place) % 128
    turned = pltpu.roll(coarse, shift, 1)
    turned_far = pltpu.roll(turned, 64, 1)
    rows[...] = jnp.broadcast_to(turned[0:1] + turned_far[1:2], (LAYER, 128))


def repack_kernel(rows, out, packed):
    taken = rows[...]
    far = pltpu.roll(taken, 64, 1)
    place = lax.broadcasted_iota(jnp.int32, (LAYER, 128), 0)
    lane = lax.broadcasted_iota(jnp.int32, (LAYER, 128), 1)
    within = (lane - NV * place + NV * LAYER) & 127
    row = jnp.where(within < NV, (NV * (place & 15) + within) >> 7, -1)
    for load, field in enumerate((taken, far)):
        for r in range(3):
            kept = jnp.where(row == r, field, 0.0)
            for group in range(2):
                packed[load * 6 + group * 3 + r : load * 6 + group * 3 + r + 1, :] = jnp.sum(
                    kept[group * 16 : (group + 1) * 16], axis=0, keepdims=True
                )
    whole = packed[...]
    for z in range(Z):
        out[z] = whole


def partial_kernel(gathered, mine, given, rounded, held, weights, mask, shared, local):
    first = lax.axis_index("c") == 0
    sums = [[[jnp.zeros((NV, 128), F32) for _ in range(2)] for _ in range(2)] for _ in range(2)]
    for t in range(HALF // 128):
        z, r = divmod(t, 6)
        blocks = [rows[:, t * 128 : (t + 1) * 128] for rows in (mine, given)]
        for load in range(2):
            factor = gathered[z, load * 6 + r : load * 6 + r + 1, :]
            for owner in range(2):
                sums[owner][load][t % 2] += blocks[owner] * factor
    lane = lax.broadcasted_iota(jnp.int32, (NV, 128), 1)
    tile = jnp.zeros((NV, 128), F32)
    for owner in range(2):
        at = jnp.where(first, 2 * owner, 2 - 2 * owner)
        for load in range(2):
            part = jnp.sum(sums[owner][load][0] + sums[owner][load][1], axis=1, keepdims=True)
            tile = jnp.where(lane == at + load, part, tile)
    shared[:NV] = tile
    weighted = weight_row(weights) * mask[...] * jnp.dot(rounded[...], held[...], preferred_element_type=F32)
    local[...] = weighted
    for load in range(2):
        for half in range(2):
            at = NV + 2 * load + half
            shared[at : at + 1, :] = weighted[load : load + 1, half * H : (half + 1) * H]
    shared[NV + 4 :] = jnp.zeros((4, 128), F32)


def coarse_kernel(shared, local, basis, weights, mask, given, before, correction, both):
    first = lax.axis_index("c") == 0
    total = shared[:NV] + shared[32 : 32 + NV]
    total = total.astype(BF16).astype(F32)
    vectors = basis[...].astype(F32)
    partner_local = jnp.where(first, shared[56:60], shared[24:28])
    fixes, partner = [], []
    for load in range(2):
        pair = [total[:, load : load + 1], total[:, 2 + load : 3 + load]]
        coarse = jnp.where(first, pair[0], pair[1])
        fixes.append(jnp.sum(vectors * coarse, axis=0, keepdims=True))
        coarse = jnp.where(first, pair[1], pair[0])
        term = jnp.sum(given[:, HALF:] * coarse, axis=0, keepdims=True)
        halves = [
            partner_local[2 * load + half : 2 * load + half + 1, :] + term[:, half * H : (half + 1) * H]
            for half in range(2)
        ]
        partner.append(jnp.concatenate(halves, axis=1))
    value = local[...] + weight_row(weights) * mask[...] * jnp.concatenate(fixes, axis=0)
    correction[...] = value
    low = [before[6 + j // 2, j % 2 : j % 2 + 1, :].astype(jnp.int32) for j in range(6)]
    high = [before[15 + j // 2, j % 2 : j % 2 + 1, :].astype(jnp.int32) for j in range(6)]
    select = selection_of([jnp.where(first, low[j], high[j]) for j in range(6)])
    partner_select = selection_of([jnp.where(first, high[j], low[j]) for j in range(6)])
    own = times_selection(value[:, :EDGE], jnp.concatenate(select, axis=1))
    other = times_selection(jnp.concatenate(partner, axis=0), jnp.concatenate(partner_select, axis=1))
    for j in range(6):
        mine, theirs = own[:, j * H : (j + 1) * H], other[:, j * H : (j + 1) * H]
        both[j] = jnp.where(first, mine, theirs)
        both[6 + j] = jnp.where(first, theirs, mine)


def last_kernel(iterate, correction, both, moved, spread, solved):
    arrived = times_selection(arrivals(both, moved), spread[...])
    value = iterate[...] + correction[...]
    solved[...] = value
    solved[:, :EDGE] = value[:, :EDGE] + arrived


def per_device(
    rhs, start, stiffness, local_inverse, basis, weights, coarse_inverse, orders, out_rows, out_counts, in_rows
):
    out_rows = out_rows.reshape(6, 1, H)
    in_rows = in_rows.reshape(6, 1, H)
    weights = weights.reshape(6, 128)
    edge, mask, iterate, own, beyond, arriving = on_chip(
        first_kernel,
        [
            ((2, EDGE), F32),
            ((1, N), F32),
            ((2, N), F32),
            ((9, 2, H), F32),
            ((N, N - EDGE), BF16),
            ((6, 1, H), jnp.int32),
        ],
        [start, stiffness, orders, out_rows, out_counts, in_rows],
        far=(0, 1, 3, 4, 5),
        work=pl.CostEstimate(flops=2 * 10**9, transcendentals=0, bytes_accessed=1 << 21),
        loose=(2,),
        scratch=[
            pltpu.VMEM((N, EDGE), BF16),
            pltpu.VMEM((2, N), F32),
            pltpu.VMEM((6, 1, H), jnp.int32),
            pltpu.SMEM((1,), jnp.int32),
            pltpu.SMEM((1, 6), jnp.int32),
            pltpu.SemaphoreType.DMA((7,)),
        ],
    )
    both = in_pair(own)
    going = across(both)
    spread, rest, mine, theirs = on_chip(
        rest_kernel,
        [((6 * H, EDGE), BF16), ((2, N - EDGE), F32), ((NV, HALF), F32), ((NV, HALF + EDGE), F32)],
        [iterate, beyond, mask, weights, basis, coarse_inverse, arriving],
    )
    given = lax.ppermute(theirs, "c", [(0, 1), (1, 0)])
    before = both
    moved = in_pair(jnp.concatenate(going))
    residual, rounded, rows = on_chip(
        residual_kernel,
        [((2, N), F32), ((2, N), BF16), ((LAYER, 128), F32)],
        [edge, rest, both, moved, spread, rhs, mask, basis],
    )
    rows = lax.all_to_all(rows.reshape(LAYER, 1, 128), ("y", "x"), 0, 0).reshape(LAYER, 128)
    (gathered,) = on_chip(repack_kernel, [((Z, 12, 128), F32)], [rows], scratch=[pltpu.VMEM((12, 128), F32)])
    gathered = lax.all_to_all(gathered, "z", 0, 0)
    shared, local = on_chip(
        partial_kernel,
        [((32, 128), F32), ((2, N), F32)],
        [gathered, mine, given, rounded, local_inverse, weights, mask],
    )
    correction, both = on_chip(
        coarse_kernel,
        [((2, N), F32), ((12, 2, H), F32)],
        [in_pair(shared), local, basis, weights, mask, given, before],
    )
    moved = in_pair(jnp.concatenate(across(both)))
    (solved,) = on_chip(last_kernel, [((2, N), F32)], [iterate, correction, both, moved, spread])
    return solved, residual


def solution(mesh):
    fine = Mesh(mesh.devices.reshape(Z, Y, C, X), ALL)
    return jax.shard_map(
        per_device,
        mesh=fine,
        in_specs=(
            P(None, ALL),
            P(None, ALL),
            P(ALL, None),
            P(ALL, None),
            P(None, ALL),
            P(ALL),
            P(ALL, None),
            P(ALL),
            P(ALL, None, None),
            P(ALL, None),
            P(ALL, None, None),
        ),
        out_specs=(P(None, ALL), P(None, ALL)),
        check_vma=False,
    )
```

```python
import jax
import jax.numpy as jnp
from jax import lax
from jax.experimental import pallas as pl
from jax.experimental.pallas import tpu as pltpu
from jax.sharding import Mesh
from jax.sharding import PartitionSpec as P

Z, Y, C, X = 12, 8, 2, 4
LAYER = Y * X
HALF = Z * LAYER * 24
N = 768
NV = 24
H = 128
EDGE = 256
F32, BF16 = jnp.float32, jnp.bfloat16
ALL = ("z", "y", "c", "x")
CHIPS = ("z", "y", "c")
LEAN = pltpu.CompilerParams(vmem_limit_bytes=8 << 20)


def on_chip(kernel, out_shape, args, far=(), scratch=(), loose=(), work=None, place=pltpu.VMEM):
    spaces = [pl.ANY if i in loose else pltpu.HBM if i in far else pltpu.VMEM for i in range(len(args))]
    args = [a if i in loose else pltpu.with_memory_space_constraint(a, spaces[i]) for i, a in enumerate(args)]
    return pl.pallas_call(
        kernel,
        in_specs=[pl.BlockSpec(memory_space=space) for space in spaces],
        out_specs=[pl.BlockSpec(memory_space=place)] * len(out_shape),
        out_shape=[place(shape, dtype) for shape, dtype in out_shape],
        scratch_shapes=list(scratch),
        compiler_params=LEAN,
        cost_estimate=work,
    )(*args)


def thirds(value):
    high = value.astype(BF16)
    rest = value - high.astype(F32)
    middle = rest.astype(BF16)
    low = (rest - middle.astype(F32)).astype(BF16)
    return jnp.concatenate([high, middle, low], axis=0)


def times_selection(value, selection):
    parts = jnp.dot(thirds(value), selection, preferred_element_type=F32)
    return parts[0:2] + parts[2:4] + parts[4:6]


def selection_of(listed):
    rows = lax.broadcasted_iota(jnp.int32, (EDGE, H), 0)
    return [(rows == one).astype(F32).astype(BF16) for one in listed]


def spread_of(arriving):
    rows = lax.broadcasted_iota(jnp.int32, (EDGE, H), 0)
    return jnp.concatenate([(rows == arriving[j]).astype(F32).T.astype(BF16) for j in range(6)], axis=0)


def arrivals(both, moved):
    first = lax.axis_index("c") == 0
    up, down, second = 0, moved.shape[0] // 2, both.shape[0] // 2
    return jnp.concatenate(
        [
            jnp.where(first, moved[up + 3], moved[up + 4]),
            jnp.where(first, moved[down + 3], moved[down + 4]),
            jnp.where(first, moved[up + 2], both[2]),
            jnp.where(first, both[second + 3], moved[down + 2]),
            jnp.where(first, moved[up], moved[up + 1]),
            jnp.where(first, moved[down], moved[down + 1]),
        ],
        axis=1,
    )


def across(both):
    chips = Z * Y
    first = lax.axis_index("c") == 0
    own, other = both[: both.shape[0] // 2], both[both.shape[0] // 2 :]
    along_x = jnp.where(first, jnp.stack([own[0], other[0]]), jnp.stack([own[1], other[1]]))
    along_y = jnp.where(first, jnp.stack([own[4], other[4], other[2]]), jnp.stack([own[5], other[5], own[3]]))
    route_y = [(2 * q, 2 * q + 2) for q in range(chips - 1)] + [(2 * q + 1, 2 * q - 1) for q in range(1, chips)]
    route_x = [(d, d + 1) for d in range(X - 1)] + [(X + d, X + d - 1) for d in range(1, X)]
    got_y = lax.ppermute(along_y, CHIPS, route_y)
    got_x = lax.ppermute(along_x, ("c", "x"), route_x)
    return [got_y, got_x]


def in_pair(value):
    return lax.all_gather(value, "c", axis=0, tiled=True)


def first_kernel(
    start, stiff, orders, out_rows, counts, in_rows, edge, mask, iterate, own, beyond, arriving, columns, fields, listing, order, count, done
):
    copies = [
        pltpu.make_async_copy(counts, count, done.at[0]),
        pltpu.make_async_copy(out_rows, listing, done.at[1]),
        pltpu.make_async_copy(orders, order, done.at[2]),
        pltpu.make_async_copy(start, fields, done.at[3]),
        pltpu.make_async_copy(stiff.at[:, pl.ds(0, EDGE)], columns, done.at[4]),
        pltpu.make_async_copy(in_rows, arriving, done.at[5]),
        pltpu.make_async_copy(stiff.at[:, pl.ds(EDGE, N - EDGE)], beyond, done.at[6]),
    ]
    for copy in copies:
        copy.start()
    slots = lax.broadcasted_iota(jnp.int32, (1, H), 1)
    copies[0].wait()
    copies[1].wait()
    listed = [jnp.where(slots < count[0, j], listing[j], -1) for j in range(6)]
    select = selection_of(listed)
    for j in range(6):
        own[6 + j // 2, j % 2 : j % 2 + 1, :] = listed[j].astype(F32)
    copies[2].wait()
    kept = lax.broadcasted_iota(jnp.int32, (1, N), 1) < order[0]
    mask[...] = kept.astype(F32)
    copies[3].wait()
    masked = jnp.where(kept, fields[...], 0.0)
    iterate[...] = masked
    copies[4].wait()
    product = jnp.dot(masked.astype(BF16), columns[...], preferred_element_type=F32)
    edge[...] = product
    picked = times_selection(product, jnp.concatenate(select, axis=1))
    for j in range(6):
        own[j] = picked[:, j * H : (j + 1) * H]
    copies[5].wait()
    copies[6].wait()


def weight_row(weights):
    return jnp.concatenate([weights[j : j + 1, :] for j in range(6)], axis=1)


def rest_kernel(iterate, beyond, mask, weights, basis, inverse, arriving, spread, rest, mine, theirs):
    first = lax.axis_index("c") == 0
    spread[...] = spread_of(arriving)
    rest[...] = jnp.dot(iterate[...].astype(BF16), beyond[...], preferred_element_type=F32)
    weighted = basis[...].astype(F32) * (weight_row(weights) * mask[...])
    theirs[:, HALF:] = weighted[:, :EDGE]
    for group in range(HALF // 384):
        block = inverse[:, group * 768 : (group + 1) * 768]
        low = jnp.concatenate([block[:, k * 192 : k * 192 + 96] for k in range(4)], axis=1)
        high = jnp.concatenate([block[:, k * 192 + 96 : k * 192 + 192] for k in range(4)], axis=1)
        mine[:, group * 384 : (group + 1) * 384] = jnp.where(first, low, high)
        theirs[:, group * 384 : (group + 1) * 384] = jnp.where(first, high, low)


def residual_kernel(edge, rest, both, moved, spread, rhs, mask, basis, residual, rounded, rows):
    summed = edge[...] + times_selection(arrivals(both, moved), spread[...])
    total = jnp.concatenate([summed, rest[...]], axis=1)
    value = jnp.where(mask[...] > 0.0, rhs[...] - total, 0.0)
    residual[...] = value
    rounded[...] = value.astype(BF16)
    padded = jnp.concatenate([value, jnp.zeros((6, N), F32)], axis=0).astype(BF16)
    coarse = lax.dot_general(padded, basis[...], (((1,), (1,)), ((), ())), preferred_element_type=F32)
    coarse = jnp.concatenate([coarse, jnp.zeros((8, 128 - NV), F32)], axis=1)
    place = lax.axis_index("y") * X + lax.axis_index("x")
    shift = (24 * place) % 128
    turned = pltpu.roll(coarse, shift, 1)
    turned_far = pltpu.roll(turned, 64, 1)
    rows[...] = jnp.broadcast_to(turned[0:1] + turned_far[1:2], (LAYER, 128))


def repack_kernel(rows, out, packed):
    taken = rows[...]
    far = pltpu.roll(taken, 64, 1)
    place = lax.broadcasted_iota(jnp.int32, (LAYER, 128), 0)
    lane = lax.broadcasted_iota(jnp.int32, (LAYER, 128), 1)
    within = (lane - NV * place + NV * LAYER) & 127
    row = jnp.where(within < NV, (NV * (place & 15) + within) >> 7, -1)
    for load, field in enumerate((taken, far)):
        for r in range(3):
            kept = jnp.where(row == r, field, 0.0)
            for group in range(2):
                packed[load * 6 + group * 3 + r : load * 6 + group * 3 + r + 1, :] = jnp.sum(
                    kept[group * 16 : (group + 1) * 16], axis=0, keepdims=True
                )
    whole = packed[...]
    for z in range(Z):
        out[z] = whole


def partial_kernel(gathered, mine, given, rounded, held, weights, mask, shared, local):
    first = lax.axis_index("c") == 0
    sums = [[[jnp.zeros((NV, 128), F32) for _ in range(2)] for _ in range(2)] for _ in range(2)]
    for t in range(HALF // 128):
        z, r = divmod(t, 6)
        blocks = [rows[:, t * 128 : (t + 1) * 128] for rows in (mine, given)]
        for load in range(2):
            factor = gathered[z, load * 6 + r : load * 6 + r + 1, :]
            for owner in range(2):
                sums[owner][load][t % 2] += blocks[owner] * factor
    lane = lax.broadcasted_iota(jnp.int32, (NV, 128), 1)
    tile = jnp.zeros((NV, 128), F32)
    for owner in range(2):
        at = jnp.where(first, 2 * owner, 2 - 2 * owner)
        for load in range(2):
            part = jnp.sum(sums[owner][load][0] + sums[owner][load][1], axis=1, keepdims=True)
            tile = jnp.where(lane == at + load, part, tile)
    shared[:NV] = tile
    weighted = weight_row(weights) * mask[...] * jnp.dot(rounded[...], held[...], preferred_element_type=F32)
    local[...] = weighted
    for load in range(2):
        for half in range(2):
            at = NV + 2 * load + half
            shared[at : at + 1, :] = weighted[load : load + 1, half * H : (half + 1) * H]
    shared[NV + 4 :] = jnp.zeros((4, 128), F32)


def coarse_kernel(shared, local, basis, weights, mask, given, before, correction, both):
    first = lax.axis_index("c") == 0
    total = shared[:NV] + shared[32 : 32 + NV]
    total = total.astype(BF16).astype(F32)
    vectors = basis[...].astype(F32)
    partner_local = jnp.where(first, shared[56:60], shared[24:28])
    fixes, partner = [], []
    for load in range(2):
        pair = [total[:, load : load + 1], total[:, 2 + load : 3 + load]]
        coarse = jnp.where(first, pair[0], pair[1])
        fixes.append(jnp.sum(vectors * coarse, axis=0, keepdims=True))
        coarse = jnp.where(first, pair[1], pair[0])
        term = jnp.sum(given[:, HALF:] * coarse, axis=0, keepdims=True)
        halves = [
            partner_local[2 * load + half : 2 * load + half + 1, :] + term[:, half * H : (half + 1) * H]
            for half in range(2)
        ]
        partner.append(jnp.concatenate(halves, axis=1))
    value = local[...] + weight_row(weights) * mask[...] * jnp.concatenate(fixes, axis=0)
    correction[...] = value
    low = [before[6 + j // 2, j % 2 : j % 2 + 1, :].astype(jnp.int32) for j in range(6)]
    high = [before[15 + j // 2, j % 2 : j % 2 + 1, :].astype(jnp.int32) for j in range(6)]
    select = selection_of([jnp.where(first, low[j], high[j]) for j in range(6)])
    partner_select = selection_of([jnp.where(first, high[j], low[j]) for j in range(6)])
    own = times_selection(value[:, :EDGE], jnp.concatenate(select, axis=1))
    other = times_selection(jnp.concatenate(partner, axis=0), jnp.concatenate(partner_select, axis=1))
    for j in range(6):
        mine, theirs = own[:, j * H : (j + 1) * H], other[:, j * H : (j + 1) * H]
        both[j] = jnp.where(first, mine, theirs)
        both[6 + j] = jnp.where(first, theirs, mine)


def last_kernel(iterate, correction, both, moved, spread, solved, value, done):
    value[:, EDGE:] = iterate[:, EDGE:] + correction[:, EDGE:]
    far = pltpu.make_async_copy(value.at[:, pl.ds(EDGE, N - EDGE)], solved.at[:, pl.ds(EDGE, N - EDGE)], done.at[0])
    far.start()
    arrived = times_selection(arrivals(both, moved), spread[...])
    value[:, :EDGE] = iterate[:, :EDGE] + correction[:, :EDGE] + arrived
    near = pltpu.make_async_copy(value.at[:, pl.ds(0, EDGE)], solved.at[:, pl.ds(0, EDGE)], done.at[1])
    near.start()
    far.wait()
    near.wait()


def per_device(
    rhs, start, stiffness, local_inverse, basis, weights, coarse_inverse, orders, out_rows, out_counts, in_rows
):
    out_rows = out_rows.reshape(6, 1, H)
    in_rows = in_rows.reshape(6, 1, H)
    weights = weights.reshape(6, 128)
    edge, mask, iterate, own, beyond, arriving = on_chip(
        first_kernel,
        [
            ((2, EDGE), F32),
            ((1, N), F32),
            ((2, N), F32),
            ((9, 2, H), F32),
            ((N, N - EDGE), BF16),
            ((6, 1, H), jnp.int32),
        ],
        [start, stiffness, orders, out_rows, out_counts, in_rows],
        far=(0, 1, 3, 4, 5),
        work=pl.CostEstimate(flops=2 * 10**9, transcendentals=0, bytes_accessed=1 << 21),
        loose=(2,),
        scratch=[
            pltpu.VMEM((N, EDGE), BF16),
            pltpu.VMEM((2, N), F32),
            pltpu.VMEM((6, 1, H), jnp.int32),
            pltpu.SMEM((1,), jnp.int32),
            pltpu.SMEM((1, 6), jnp.int32),
            pltpu.SemaphoreType.DMA((7,)),
        ],
    )
    both = in_pair(own)
    going = across(both)
    spread, rest, mine, theirs = on_chip(
        rest_kernel,
        [((6 * H, EDGE), BF16), ((2, N - EDGE), F32), ((NV, HALF), F32), ((NV, HALF + EDGE), F32)],
        [iterate, beyond, mask, weights, basis, coarse_inverse, arriving],
    )
    given = lax.ppermute(theirs, "c", [(0, 1), (1, 0)])
    before = both
    moved = in_pair(jnp.concatenate(going))
    residual, rounded, rows = on_chip(
        residual_kernel,
        [((2, N), F32), ((2, N), BF16), ((LAYER, 128), F32)],
        [edge, rest, both, moved, spread, rhs, mask, basis],
    )
    rows = lax.all_to_all(rows.reshape(LAYER, 1, 128), ("y", "x"), 0, 0).reshape(LAYER, 128)
    (gathered,) = on_chip(repack_kernel, [((Z, 12, 128), F32)], [rows], scratch=[pltpu.VMEM((12, 128), F32)])
    gathered = lax.all_to_all(gathered, "z", 0, 0)
    shared, local = on_chip(
        partial_kernel,
        [((32, 128), F32), ((2, N), F32)],
        [gathered, mine, given, rounded, local_inverse, weights, mask],
    )
    correction, both = on_chip(
        coarse_kernel,
        [((2, N), F32), ((12, 2, H), F32)],
        [in_pair(shared), local, basis, weights, mask, given, before],
    )
    moved = in_pair(jnp.concatenate(across(both)))
    (solved,) = on_chip(last_kernel, [((2, N), F32)], [iterate, correction, both, moved, spread], place=pltpu.HBM, scratch=[pltpu.VMEM((2, N), F32), pltpu.SemaphoreType.DMA((2,))])
    return solved, residual


def solution(mesh):
    fine = Mesh(mesh.devices.reshape(Z, Y, C, X), ALL)
    return jax.shard_map(
        per_device,
        mesh=fine,
        in_specs=(
            P(None, ALL),
            P(None, ALL),
            P(ALL, None),
            P(ALL, None),
            P(None, ALL),
            P(ALL),
            P(ALL, None),
            P(ALL),
            P(ALL, None, None),
            P(ALL, None),
            P(ALL, None, None),
        ),
        out_specs=(P(None, ALL), P(None, ALL)),
        check_vma=False,
    )
```
